32 devices in a mesh: dp: 8 (over z, y), tensor: 4 (over x, core).
Axes of the slice: x: 2, y: 2, z: 4, core: 2. Of those that a mesh axis runs over, the one named last changes fastest.
Arguments:
- hidden: bfloat16 [128, 4608], P('dp'), may hold values from -6 to 6
- tied_table: bfloat16 [16384, 4608], P(('dp', 'tensor')), may hold values from -0.25 to 0.25
- targets: int32 [128], P('dp'), may hold values from 0 to 16383
- loss_weight: bfloat16 [128], P('dp'), may hold values from 2 to 20
- inputs: int32 [128], P('dp'), may hold values from 0 to 16383
- embed_grad: bfloat16 [128, 4608], P('dp'), may hold values from -0.09375 to 0.09375
Outputs:
- table_grad: bfloat16 [16384, 4608], P(('dp', 'tensor'))
- hidden_grad: float32 [128, 4608], P('dp', 'tensor')
The draws below stay inside these ranges and needn't reach their ends.
All inputs are finite; a program needn't handle non-finite values.
Results may differ from the reference program's by a relative error of at most 0.0052.
Values may be sent and summed in bfloat16 or wider, within the bound.
A program may use at most 64 MiB of HBM per device.

```python
import math
import jax
import jax.numpy as jnp
import numpy as np
from jax import lax

D = 4608
VOCAB = 16384
TOKENS = 128
N_DP = 8


def place_ends(entries, rng, low, largest):
    spot = [jax.random.randint(jax.random.fold_in(rng, axis), (), 0, length) for axis, length in enumerate(entries.shape)]
    longest = entries.shape.index(max(entries.shape))
    neighbour = spot[:longest] + [(spot[longest] + 1) % entries.shape[longest]] + spot[longest + 1:]
    return entries.at[tuple(spot)].set(low).at[tuple(neighbour)].set(largest)


def shard_levels(rng, extent, split, least, largest):
    loudness = 1.0
    for position, parts in split:
        steps = jax.random.uniform(jax.random.fold_in(jax.random.fold_in(rng, 6), position), (parts,), jnp.float32, least / len(split), largest / len(split))
        loudness = loudness * jnp.repeat(jnp.exp(steps), extent[position] // parts).reshape((-1,) + (1,) * (len(extent) - 1 - position))
    return loudness


def cumulative_ranks(amount, lean):
    weights = [(1 << 20) // math.isqrt(rank ** lean) + 1 for rank in range(1, amount + 1)]
    scale = 1 + sum(weights) // (1 << 30)
    return np.cumsum(np.array([max(1, weight // scale) for weight in weights]))


def skewed_ids(stream_key, dims, amount, lean):
    grid = cumulative_ranks(amount, lean)
    pick = jax.random.randint(jax.random.fold_in(stream_key, 1), dims, 0, int(grid[amount - 1]))
    grade = jnp.searchsorted(jnp.asarray(grid, jnp.int32), pick, side="right")
    return jax.random.permutation(jax.random.fold_in(stream_key, 2), amount)[grade].astype(jnp.int32)


def normal_values(stream_key, shape, deviation, reach, split=(), dtype=jnp.bfloat16):
    gain = shard_levels(stream_key, shape, split, -0.22, 0.18) if split else 1.0
    values = jax.random.normal(stream_key, shape, jnp.float32) * deviation * gain
    return jnp.minimum(jnp.maximum(values, -reach), reach).astype(dtype)


def setup_inputs(seed: int = 0) -> dict:
    seeds = jax.random.split(jax.random.key(seed), 7)
    hidden = normal_values(seeds[0], (TOKENS, D), 1.0, 6.0, ((0, 8),))
    tied_table = normal_values(seeds[1], (VOCAB, D), (D // 9) ** -0.5, 0.25, ((0, 32),))
    targets = place_ends(skewed_ids(seeds[2], (TOKENS,), VOCAB, 2), jax.random.fold_in(seeds[2], 3), 0, VOCAB - 1).astype(jnp.int32)
    loss_weight = jnp.clip(jnp.exp(math.log(20.0) - 2.3025851 * jax.random.uniform(seeds[3], (TOKENS,), jnp.float32) ** shard_levels(seeds[3], (TOKENS,), ((0, 8),), -0.2, 0.2)), 2.0, 20.0).astype(jnp.bfloat16)
    inputs = place_ends(skewed_ids(seeds[4], (TOKENS,), VOCAB, 2), jax.random.fold_in(seeds[4], 3), 0, VOCAB - 1).astype(jnp.int32)
    embed_grad = normal_values(seeds[5], (TOKENS, D), D ** -0.5, 0.09375, ((0, 8),))
    return dict(hidden=hidden, tied_table=tied_table, targets=targets, loss_weight=loss_weight, inputs=inputs, embed_grad=embed_grad)


def capped_block(hidden, tied_table, block_index, block_size):
    start = (block_index * block_size).astype(jnp.int32)
    piece = lax.dynamic_slice_in_dim(tied_table, start, block_size, 0)
    logits = lax.dot_general(hidden, piece, (((1,), (1,)), ((), ())), preferred_element_type=jnp.float32)
    return (piece, jnp.tanh(logits / 30.0))

def reference(hidden, tied_table, targets, loss_weight, inputs, embed_grad):
    token_count = hidden.shape[0]
    width = hidden.shape[1]
    vocab_size = tied_table.shape[0]
    block_size = vocab_size // N_DP
    indices = jnp.arange(N_DP).astype(jnp.int32)

    def add_exp(carry, block_index):
        unused, squash = capped_block(hidden, tied_table, block_index, block_size)
        return (carry + lax.optimization_barrier(jnp.sum(jnp.exp(30.0 * squash), axis=1)), None)
    total, unused = lax.scan(add_exp, jnp.zeros((token_count,), jnp.float32), indices)
    weights = loss_weight.astype(jnp.float32)

    def backward(carry, block_index):
        piece, squash = capped_block(hidden, tied_table, block_index, block_size)
        columns = (block_index * block_size + jnp.arange(block_size)).astype(jnp.int32)
        hits = (targets[:, None] == columns[None, :]).astype(jnp.float32)
        probs = jnp.exp(30.0 * squash) / total[:, None]
        dlogit = (weights[:, None] * (probs - hits) * (1.0 - squash * squash)).astype(jnp.bfloat16)
        carry = carry + jnp.dot(dlogit, piece, preferred_element_type=jnp.float32)
        head_term = lax.dot_general(dlogit, hidden, (((0,), (0,)), ((), ())), preferred_element_type=jnp.float32)
        onehot = (inputs[None, :] == columns[:, None]).astype(jnp.bfloat16)
        embed_term = jnp.dot(onehot, embed_grad, preferred_element_type=jnp.float32)
        return (carry, (head_term + math.sqrt(width) * embed_term).astype(jnp.bfloat16))
    hidden_grad, stacked = lax.scan(backward, jnp.zeros((token_count, width), jnp.float32), indices)
    return (stacked.reshape(vocab_size, width), hidden_grad)
```

```python
import functools
import math

import jax
import jax.numpy as jnp
from jax import lax
from jax.experimental import pallas as pl
from jax.experimental.pallas import tpu as pltpu
from jax.sharding import PartitionSpec as P

MESH = pl.DeviceIdType.MESH
LANES = (((1,), (1,)), ((), ()))


def kernel(
    n_dp, n_t, scale,
    targets, inputs, weights, hid, emb, table, tg, hg,
    tgt, inp, wts, hb, eb, ma, ids, tab, sq, dl, oh, dlt, sv, sd, pf, pb, r0, qa, ra, qb, rb, q2a, r2a, q2b, r2b,
    acc, q3a, r3a, q3b, r3b, span, ss, rs, ls,
):
    d, t = lax.axis_index("dp"), lax.axis_index("tensor")
    n_a, n_x = n_dp // 2, n_t // 2
    a, b = lax.div(d, 2), lax.rem(d, 2)
    x, c = lax.div(t, 2), lax.rem(t, 2)
    e = lax.rem(x, 2)
    rows, width = hid.shape
    tokens = n_dp * rows
    vocab = tab.shape[0]
    half, quarter, cols = width // 2, width // 4, width // n_t
    f32, bf16 = jnp.float32, jnp.bfloat16
    others = range(1, n_a)
    low = a < n_a // 2

    xs = [x] + [lax.rem(x + j, n_x) for j in range(1, n_x)]
    side, sib, across = (a * 2 + 1 - b, t), (d, x * 2 + 1 - c), (d, (x + 1 - 2 * e) * 2 + c)
    near_slot = [0] + [jnp.where(low, p, n_a - p) for p in others]
    far_slot = [0] + [jnp.where(low, n_a - p, p) for p in others]
    ups = [a] + [lax.rem(a + near_slot[p], n_a) for p in others]

    barrier = pltpu.get_barrier_semaphore()
    greet = [(ups[p] * 2 + b, t) for p in others] + [side, across, sib]
    for u in range(2, n_x):
        pair = lax.rem(x - e + u, n_x)
        for dp in range(n_dp):
            for k in range(2):
                if u % 2 == 0:
                    greet += [(dp, (pair + i) * 2 + k) for i in range(2)]
    for dev in greet:
        pl.semaphore_signal(barrier, inc=1, device_id=dev, device_id_type=MESH)

    loads = [
        pltpu.make_async_copy(hid, hb.at[0, 0], ls.at[0]),
        pltpu.make_async_copy(emb, eb.at[0, 0], ls.at[1]),
        pltpu.make_async_copy(table, tab, ls.at[2]),
        pltpu.make_async_copy(targets, tgt, ls.at[3]),
        pltpu.make_async_copy(inputs, inp, ls.at[4]),
        pltpu.make_async_copy(weights, wts, ls.at[5]),
    ]
    for n in (0, 3, 4, 5, 1, 2):
        loads[n].start()

    groups, total_sent = [], [0]

    def group(size=1):
        groups.append([0, size, sum(g[1] for g in groups)])
        return groups[-1]

    def send(src, dst, dev, g, at=0):
        size = math.prod(src.shape) * src.dtype.itemsize
        g[0] += size
        total_sent[0] += size
        pltpu.make_async_remote_copy(
            src_ref=src, dst_ref=dst, send_sem=ss.at[0], recv_sem=rs.at[g[2] + at], device_id=dev, device_id_type=MESH
        ).start()

    def whole(size, at):
        ref = span.at[pl.ds(0, size // 512)]
        return pltpu.make_async_remote_copy(
            src_ref=ref, dst_ref=ref, send_sem=ss.at[0], recv_sem=rs.at[at], device_id=side, device_id_type=MESH
        )

    def arrived(g, at=0, parts=1):
        whole(g[0] // parts, g[2] + at).wait_recv()

    def lanes(at, size):
        return pl.ds(pl.multiple_of(at, 128), size)

    near = lanes((c * 2 + e) * quarter, quarter)
    far = lanes((c * 2 + 1 - e) * quarter, quarter)
    mine = lanes(c * half, half)
    first = (quarter // 128 + 1) // 2 * 128
    near_a = lanes((c * 2 + e) * quarter, first)
    far_b = lanes((c * 2 + 1 - e) * quarter + first, quarter - first)

    class Gather:
        def __init__(self, buf):
            self.buf = buf
            self.z, self.y, self.x, self.own = group(n_a), group(n_a), group(n_a), group()
            self.own_x, self.both, self.s0, self.s1 = group(), group(), group(), group()

        def start(self):
            buf = self.buf
            for p in reversed(others):
                k = far_slot[p]
                send(buf.at[0, 0, :, near], buf.at[0, k, :, near], (ups[p] * 2 + b, t), self.z, k)
            send(buf.at[0, 0, :, near], buf.at[1, 0, :, near], side, self.own)

        def spread(self):
            buf = self.buf
            for p in others:
                k = near_slot[p]
                arrived(self.z, k, n_a - 1)
                send(buf.at[0, k, :, near], buf.at[0, k, :, near], across, self.x, p)
                send(buf.at[0, k, :, near], buf.at[1, k, :, near], side, self.y, p)
            arrived(self.own)
            send(buf.at[1, 0, :, near], buf.at[1, 0, :, near], across, self.both)

        def cross(self):
            buf = self.buf
            for p in others:
                k = near_slot[p]
                arrived(self.x, p, n_a - 1)
                send(buf.at[0, k, :, far_b], buf.at[1, k, :, far_b], side, self.both)
                arrived(self.y, p, n_a - 1)
                send(buf.at[1, k, :, near_a], buf.at[1, k, :, near_a], across, self.both)
            send(buf.at[0, 1:n_a, :, mine], buf.at[0, 1:n_a, :, mine], sib, self.s0)
            send(buf.at[1, :, :, near], buf.at[1, :, :, near], sib, self.s0)

        def close(self):
            buf = self.buf
            arrived(self.both)
            send(buf.at[1, :, :, far], buf.at[1, :, :, far], sib, self.s1)

    hidden, embed = Gather(hb), Gather(eb)
    pl.semaphore_wait(barrier, len(greet))
    loads[0].wait()
    hidden.start()
    for n in (3, 4, 5):
        loads[n].wait()
    ma[0, 0] = jnp.zeros(ma.shape[2:], f32)
    ma[0, 0, :, 0:rows] = tgt[...].astype(f32)
    ma[0, 0, :, rows:2 * rows] = inp[...].astype(f32)
    ma[0, 0, :, 2 * rows:3 * rows] = wts[...].astype(f32)
    loads[1].wait()
    embed.start()
    hidden.spread()
    hidden.cross()
    facts = group()
    for i in range(2):
        for p in reversed(range(n_a)):
            if i + p:
                dev = (ups[p] * 2 + (1 - b if i else b), t)
                send(ma.at[0, 0], ma.at[i, far_slot[p]], dev, facts)
    loads[2].wait()
    piece = min(vocab, 256)

    def product(i, part, core):
        at = pl.ds(pl.multiple_of(i * piece, piece), piece)
        part_lanes = lanes((core * 2 + part) * quarter, quarter)
        return at, lax.dot_general(
            tab[at, part_lanes], hb[:, :, :, part_lanes].reshape(tokens, quarter), LANES, preferred_element_type=f32
        )

    def quarters(part, core, fresh=False):
        def body(i, carry):
            at, value = product(i, part, core)
            sq[at, :] = value if fresh else sq[at, :] + value
            return carry

        lax.fori_loop(0, vocab // piece, body, 0)

    def last(i, total):
        at, value = product(i, 1 - e, 1 - c)
        squash = jnp.tanh((sq[at, :] + value) / 30.0)
        sq[at, :] = squash
        return total + jnp.sum(jnp.exp(30.0 * squash), axis=0, keepdims=True)

    quarters(e, c, True)
    hidden.close()
    embed.spread()
    quarters(1 - e, c)
    arrived(hidden.s0)
    quarters(e, 1 - c)
    arrived(hidden.s1)
    part = lax.fori_loop(0, vocab // piece, last, jnp.zeros((1, tokens), f32))

    lane = lax.rem(lax.broadcasted_iota(jnp.int32, (1, tokens), 1), tokens // 2)
    for i in range(2):
        for j in range(n_a):
            move = j * rows
            value = part
            if i:
                value = pltpu.roll(value, tokens // 2, 1)
            if j:
                value = jnp.where(
                    lane < tokens // 2 - move,
                    pltpu.roll(value, tokens - move, 1),
                    pltpu.roll(value, tokens // 2 - move, 1),
                )
            sv[i * n_a + j] = value
    sums = group()
    for p in reversed(range(n_a)):
        for i in reversed(range(2)):
            for u in reversed(range(n_x)):
                for k in reversed(range(2)):
                    n = ((i * n_a + p) * n_x + u) * 2 + k
                    if n:
                        dev = (ups[p] * 2 + (1 - b if i else b), xs[u] * 2 + (1 - c if k else c))
                        row = sv.at[i * n_a + near_slot[p]]
                        send(row, sd.at[((i * n_a + far_slot[p]) * n_x + (n_x - u) % n_x) * 2 + k], dev, sums)
    sd[0] = part
    embed.cross()
    arrived(facts)
    for i in range(2):
        for j in range(n_a):
            k = i * n_a + j
            for f in range(3):
                ids[f:f + 1, k * rows:(k + 1) * rows] = ma[i, j, :, f * rows:(f + 1) * rows]
    base = (d * n_t + t) * vocab
    column = (base + lax.broadcasted_iota(jnp.int32, (vocab, tokens), 0)).astype(f32)
    oh[...] = jnp.where(column == ids[1:2, :], 1.0, 0.0).astype(bf16)
    arrived(sums)
    total = jnp.sum(sd[...], axis=0)
    squash = sq[...]
    hits = jnp.where(column == ids[0:1, :], 1.0, 0.0)
    dlogit = ids[2:3, :] * (jnp.exp(30.0 * squash) / total - hits) * (1.0 - squash * squash)
    dl[...] = dlogit.astype(bf16)
    dlt[...] = jnp.transpose(dlogit).astype(bf16)

    cut = min((cols // 128 + 1) // 2 * 128, cols) if cols % 128 == 0 else cols
    split = cut < cols
    back = tokens // 2

    def term(k):
        if cols % 128 == 0:
            at = lanes(k * cols, cols)
            return jnp.dot(dlt[...], tab[:, at], preferred_element_type=f32)
        wide = jnp.zeros((tokens, cols), f32)
        for n in range(n_t):
            value = jnp.dot(dlt[...], tab[:, n * cols:(n + 1) * cols], preferred_element_type=f32)
            wide = jnp.where(k == n, value, wide)
        return wide

    order = list(range(1, n_x)) + [0]
    cs = [group() for u in order]
    xa1, xa0, yb1, yb0, y2a, x2b, z3a, z3b = [group() for n in range(8)]
    for u in order:
        pb[u] = term(2 * xs[u] + 1 - c).astype(bf16)
        send(pb.at[u], r0.at[u], sib, cs[u])
        pf[u] = term(2 * xs[u] + c)
    for u in order:
        arrived(cs[u])
        if u:
            for low_row, g in ((back, xa1), (0, xa0)):
                at = slice(low_row, low_row + back)
                qa[u, at] = (pf[u, at, :cut] + r0[u, at, :cut].astype(f32)).astype(bf16)
                send(qa.at[u, at], ra.at[n_x - u, at], (d, xs[u] * 2 + c), g)
        if split:
            qb[u] = (pf[u, back:, cut:] + r0[u, back:, cut:].astype(f32)).astype(bf16)
            send(qb.at[u], rb.at[u], side, yb1 if u else yb0)
    embed.close()
    step = 256

    def table_cols(i, carry):
        at = lanes(i * step, step)
        head = jnp.dot(dl[...], hb[:, :, :, at].reshape(tokens, step), preferred_element_type=f32)
        tail = jnp.dot(oh[...], eb[:, :, :, at].reshape(tokens, step), preferred_element_type=f32)
        tg[:, at] = (head + scale * tail).astype(bf16)
        return carry

    def over_x(at):
        value = pf[0, at, :cut] + r0[0, at, :cut].astype(f32)
        for u in range(1, n_x):
            value = value + ra[u, at].astype(f32)
        return value

    def over_side(u):
        return pf[u, :back, cut:] + r0[u, :back, cut:].astype(f32) + rb[u].astype(f32)

    arrived(xa1)
    q2a[...] = over_x(slice(back, tokens)).astype(bf16)
    send(q2a, r2a, side, y2a)
    if split:
        arrived(yb1)
        for u in range(1, n_x):
            q2b[u] = over_side(u).astype(bf16)
            send(q2b.at[u], r2b.at[n_x - u], (d, xs[u] * 2 + c), x2b)
    arrived(xa0)
    acc[:, :cut] = over_x(slice(0, back))
    if split:
        arrived(yb0)
        acc[:, cut:] = over_side(0)
    arrived(embed.s0)
    arrived(embed.s1)
    tiles = width // step
    early = tiles // 3
    lax.fori_loop(0, early, table_cols, 0)
    arrived(y2a)
    acc[:, :cut] = acc[:, :cut] + r2a[...].astype(f32)
    for p in reversed(others):
        k = pl.multiple_of(near_slot[p] * rows, rows)
        q3a[p] = acc[pl.ds(k, rows), :cut].astype(bf16)
        send(q3a.at[p], r3a.at[far_slot[p]], (ups[p] * 2 + b, t), z3a)
    if split:
        arrived(x2b)
        value = acc[:, cut:]
        for u in range(1, n_x):
            value = value + r2b[u].astype(f32)
        acc[:, cut:] = value
        for p in reversed(others):
            k = pl.multiple_of(near_slot[p] * rows, rows)
            q3b[p] = acc[pl.ds(k, rows), cut:].astype(bf16)
            send(q3b.at[p], r3b.at[far_slot[p]], (ups[p] * 2 + b, t), z3b)
    lax.fori_loop(early, tiles, table_cols, 0)
    arrived(z3a)
    out = acc[:rows, :cut]
    for j in others:
        out = out + r3a[j].astype(f32)
    hg[:, :cut] = out
    if split:
        arrived(z3b)
        out = acc[:rows, cut:]
        for j in others:
            out = out + r3b[j].astype(f32)
        hg[:, cut:] = out
    whole(total_sent[0], 0).wait_send()


def write(tg, hg, tg_out, hg_out, sems):
    copies = [pltpu.make_async_copy(tg, tg_out, sems.at[0]), pltpu.make_async_copy(hg, hg_out, sems.at[1])]
    for copy in copies:
        copy.start()
    for copy in copies:
        copy.wait()


def per_device(n_dp, n_t, hidden, tied_table, targets, loss_weight, inputs, embed_grad):
    rows, width = hidden.shape
    vocab = tied_table.shape[0]
    tokens, cols, n_x, n_a = n_dp * rows, width // n_t, n_t // 2, n_dp // 2
    f32, bf16 = jnp.float32, jnp.bfloat16
    vmem, hbm = pl.BlockSpec(memory_space=pltpu.VMEM), pl.BlockSpec(memory_space=pl.ANY)
    cut = min((cols // 128 + 1) // 2 * 128, cols) if cols % 128 == 0 else cols
    rest = cols - cut or 128
    receives = 2 * (3 * n_a + 5) + 2 + n_x + 8
    grads = pl.pallas_call(
        functools.partial(kernel, n_dp, n_t, math.sqrt(width)),
        out_shape=(
            pltpu.VMEM((vocab, width), bf16),
            pltpu.VMEM((rows, cols), f32),
        ),
        in_specs=[hbm] * 6,
        out_specs=(vmem, vmem),
        scratch_shapes=[
            pltpu.VMEM((1, rows), jnp.int32),
            pltpu.VMEM((1, rows), jnp.int32),
            pltpu.VMEM((1, rows), bf16),
            pltpu.VMEM((2, n_a, rows, width), bf16),
            pltpu.VMEM((2, n_a, rows, width), bf16),
            pltpu.VMEM((2, n_a, 1, 128), f32),
            pltpu.VMEM((8, tokens), f32),
            pltpu.VMEM((vocab, width), bf16),
            pltpu.VMEM((vocab, tokens), f32),
            pltpu.VMEM((vocab, tokens), bf16),
            pltpu.VMEM((vocab, tokens), bf16),
            pltpu.VMEM((tokens, vocab), bf16),
            pltpu.VMEM((n_dp, 1, tokens), f32),
            pltpu.VMEM((n_dp * n_t, 1, tokens), f32),
            pltpu.VMEM((n_x, tokens, cols), f32),
            pltpu.VMEM((n_x, tokens, cols), bf16),
            pltpu.VMEM((n_x, tokens, cols), bf16),
            pltpu.VMEM((n_x, tokens, cut), bf16),
            pltpu.VMEM((n_x, tokens, cut), bf16),
            pltpu.VMEM((n_x, tokens // 2, rest), bf16),
            pltpu.VMEM((n_x, tokens // 2, rest), bf16),
            pltpu.VMEM((tokens // 2, cut), bf16),
            pltpu.VMEM((tokens // 2, cut), bf16),
            pltpu.VMEM((n_x, tokens // 2, rest), bf16),
            pltpu.VMEM((n_x, tokens // 2, rest), bf16),
            pltpu.VMEM((tokens // 2, cols), f32),
            pltpu.VMEM((n_a, rows, cut), bf16),
            pltpu.VMEM((n_a, rows, cut), bf16),
            pltpu.VMEM((n_a, rows, rest), bf16),
            pltpu.VMEM((n_a, rows, rest), bf16),
            pltpu.VMEM((tokens * width // 32, 1, 128), f32),
            pltpu.SemaphoreType.DMA((1,)),
            pltpu.SemaphoreType.DMA((receives,)),
            pltpu.SemaphoreType.DMA((6,)),
        ],
        compiler_params=pltpu.CompilerParams(
            collective_id=0, has_side_effects=True, vmem_limit_bytes=56 << 20
        ),
    )(targets[None], inputs[None], loss_weight[None], hidden, embed_grad, tied_table)
    return pl.pallas_call(
        write,
        out_shape=(jax.ShapeDtypeStruct((vocab, width), bf16), jax.ShapeDtypeStruct((rows, cols), f32)),
        in_specs=[vmem] * 2,
        out_specs=(hbm, hbm),
        scratch_shapes=[pltpu.SemaphoreType.DMA((2,))],
        compiler_params=pltpu.CompilerParams(vmem_limit_bytes=1 << 20),
    )(*grads)


def solution(mesh):
    placed = (P("dp", None), P(("dp", "tensor"), None), P("dp"), P("dp"), P("dp"), P("dp", None))
    return jax.shard_map(
        functools.partial(per_device, mesh.shape["dp"], mesh.shape["tensor"]),
        mesh=mesh,
        in_specs=placed,
        out_specs=(P(("dp", "tensor"), None), P("dp", "tensor")),
        check_vma=False,
    )
```

```python
import functools
import math

import jax
import jax.numpy as jnp
from jax import lax
from jax.experimental import pallas as pl
from jax.experimental.pallas import tpu as pltpu
from jax.sharding import PartitionSpec as P

MESH = pl.DeviceIdType.MESH
LANES = (((1,), (1,)), ((), ()))


def kernel(
    n_dp, n_t, scale,
    targets, inputs, weights, hid, emb, table, tg, hg,
    tgt, inp, wts, gb, ma, ids, tab, tabs, sq, lhs, dlt, sv, sd, pf, qa, ra, qb, rb, q2a, r2a, q2b, r2b,
    acc, q3a, r3a, q3b, r3b, span, ss, rs, ls,
):
    d, t = lax.axis_index("dp"), lax.axis_index("tensor")
    n_a, n_x = n_dp // 2, n_t // 2
    a, b = lax.div(d, 2), lax.rem(d, 2)
    x, c = lax.div(t, 2), lax.rem(t, 2)
    e = lax.rem(x, 2)
    rows, width = hid.shape
    tokens = n_dp * rows
    vocab = tab.shape[0]
    half, quarter, cols = width // 2, width // 4, width // n_t
    f32, bf16 = jnp.float32, jnp.bfloat16
    hb, eb = gb.at[0], gb.at[1]
    others = range(1, n_a)
    low = a < n_a // 2

    xs = [x] + [lax.rem(x + j, n_x) for j in range(1, n_x)]
    side, sib, across = (a * 2 + 1 - b, t), (d, x * 2 + 1 - c), (d, (x + 1 - 2 * e) * 2 + c)
    near_slot = [0] + [jnp.where(low, p, n_a - p) for p in others]
    far_slot = [0] + [jnp.where(low, n_a - p, p) for p in others]
    ups = [a] + [lax.rem(a + near_slot[p], n_a) for p in others]

    barrier = pltpu.get_barrier_semaphore()
    greet = [(ups[p] * 2 + b, t) for p in others] + [side, across, sib]
    for u in range(2, n_x):
        pair = lax.rem(x - e + u, n_x)
        for dp in range(n_dp):
            for k in range(2):
                if u % 2 == 0:
                    greet += [(dp, (pair + i) * 2 + k) for i in range(2)]
    for dev in greet:
        pl.semaphore_signal(barrier, inc=1, device_id=dev, device_id_type=MESH)

    loads = [
        pltpu.make_async_copy(hid, hb.at[0, 0], ls.at[0]),
        pltpu.make_async_copy(emb, eb.at[0, 0], ls.at[1]),
        pltpu.make_async_copy(table, tab, ls.at[2]),
        pltpu.make_async_copy(targets, tgt, ls.at[3]),
        pltpu.make_async_copy(inputs, inp, ls.at[4]),
        pltpu.make_async_copy(weights, wts, ls.at[5]),
    ]
    for n in (0, 3, 4, 5, 1, 2):
        loads[n].start()

    groups, total_sent = [], [0]

    def group(size=1):
        groups.append([0, size, sum(g[1] for g in groups)])
        return groups[-1]

    def send(src, dst, dev, g, at=0):
        size = math.prod(src.shape) * src.dtype.itemsize
        g[0] += size
        total_sent[0] += size
        pltpu.make_async_remote_copy(
            src_ref=src, dst_ref=dst, send_sem=ss.at[0], recv_sem=rs.at[g[2] + at], device_id=dev, device_id_type=MESH
        ).start()

    def whole(size, at):
        ref = span.at[pl.ds(0, size // 512)]
        return pltpu.make_async_remote_copy(
            src_ref=ref, dst_ref=ref, send_sem=ss.at[0], recv_sem=rs.at[at], device_id=side, device_id_type=MESH
        )

    def arrived(g, at=0, parts=1):
        whole(g[0] // parts, g[2] + at).wait_recv()

    def lanes(at, size):
        return pl.ds(pl.multiple_of(at, 128), size)

    near = lanes((c * 2 + e) * quarter, quarter)
    far = lanes((c * 2 + 1 - e) * quarter, quarter)
    mine = lanes(c * half, half)
    first = (quarter // 128 + 1) // 2 * 128
    near_a = lanes((c * 2 + e) * quarter, first)
    far_b = lanes((c * 2 + 1 - e) * quarter + first, quarter - first)

    class Gather:
        def __init__(self, buf):
            self.buf = buf
            self.z, self.y, self.x, self.own = group(n_a), group(n_a), group(n_a), group()
            self.own_x, self.both, self.s0, self.s1 = group(), group(), group(), group()

        def start(self):
            buf = self.buf
            for p in reversed(others):
                k = far_slot[p]
                send(buf.at[0, 0, :, near], buf.at[0, k, :, near], (ups[p] * 2 + b, t), self.z, k)

        def own_side(self):
            send(self.buf.at[0, 0, :, near], self.buf.at[1, 0, :, near], side, self.own)

        def spread(self, which):
            buf = self.buf
            for p in which:
                k = near_slot[p]
                arrived(self.z, k, n_a - 1)
                send(buf.at[0, k, :, near], buf.at[0, k, :, near], across, self.x, p)
                send(buf.at[0, k, :, near], buf.at[1, k, :, near], side, self.y, p)

        def own_across(self):
            buf = self.buf
            arrived(self.own)
            send(buf.at[1, 0, :, near], buf.at[1, 0, :, near], across, self.both)

        def cross(self):
            buf = self.buf
            for p in others:
                k = near_slot[p]
                arrived(self.x, p, n_a - 1)
                send(buf.at[0, k, :, far_b], buf.at[1, k, :, far_b], side, self.both)
                arrived(self.y, p, n_a - 1)
                send(buf.at[1, k, :, near_a], buf.at[1, k, :, near_a], across, self.both)
            send(buf.at[0, 1:n_a, :, mine], buf.at[0, 1:n_a, :, mine], sib, self.s0)
            send(buf.at[1, :, :, near], buf.at[1, :, :, near], sib, self.s0)

        def close(self):
            buf = self.buf
            arrived(self.both)
            send(buf.at[1, :, :, far], buf.at[1, :, :, far], sib, self.s1)

    hidden, embed = Gather(hb), Gather(eb)
    pl.semaphore_wait(barrier, len(greet))
    loads[0].wait()
    hidden.start()
    hidden.own_side()
    aligned = cols % 128 == 0
    shared, squashed = group(), group()
    if aligned:
        for u in range(n_x):
            send(table.at[:, lanes((2 * u + 1 - c) * cols, cols)], tabs.at[u], sib, shared)
    else:
        send(table, tabs.at[0], sib, shared)
    for n in (3, 4, 5):
        loads[n].wait()
    ma[0, 0] = jnp.zeros(ma.shape[2:], f32)
    ma[0, 0, :, 0:rows] = tgt[...].astype(f32)
    ma[0, 0, :, rows:2 * rows] = inp[...].astype(f32)
    ma[0, 0, :, 2 * rows:3 * rows] = wts[...].astype(f32)
    hidden.spread(others)
    hidden.own_across()
    loads[1].wait()
    embed.start()
    hidden.cross()
    facts = group()
    for i in range(2):
        for p in reversed(range(n_a)):
            if i + p:
                dev = (ups[p] * 2 + (1 - b if i else b), t)
                send(ma.at[0, 0], ma.at[i, far_slot[p]], dev, facts)
    loads[2].wait()
    piece = min(vocab, 256)

    def product(i, part, core):
        at = pl.ds(i * piece, piece)
        part_lanes = lanes((core * 2 + part) * quarter, quarter)
        return at, lax.dot_general(
            tab[at, part_lanes], hb[:, :, :, part_lanes].reshape(tokens, quarter), LANES, preferred_element_type=f32
        )

    def quarters(part, core, fresh=False):
        for i in range(vocab // piece):
            at, value = product(i, part, core)
            sq[0, at, :] = value if fresh else sq[0, at, :] + value

    def last(i, total):
        at, value = product(i, 1 - e, 1 - c)
        squash = jnp.tanh((sq[0, at, :] + value) / 30.0)
        sq[0, at, :] = squash
        return total + jnp.sum(jnp.exp(30.0 * squash), axis=0, keepdims=True)

    quarters(e, c, True)
    hidden.close()
    embed.own_side()
    embed.spread(others[:2])
    quarters(1 - e, c)
    arrived(hidden.s0)
    quarters(e, 1 - c)
    arrived(hidden.s1)
    part = jnp.zeros((1, tokens), f32)
    for i in range(vocab // piece):
        part = last(i, part)

    lane = lax.rem(lax.broadcasted_iota(jnp.int32, (1, tokens), 1), tokens // 2)
    for i in range(2):
        for j in range(n_a):
            move = j * rows
            value = part
            if i:
                value = pltpu.roll(value, tokens // 2, 1)
            if j:
                value = jnp.where(
                    lane < tokens // 2 - move,
                    pltpu.roll(value, tokens - move, 1),
                    pltpu.roll(value, tokens // 2 - move, 1),
                )
            sv[i * n_a + j] = value
    sums = group()
    for p in reversed(range(n_a)):
        for i in reversed(range(2)):
            for u in reversed(range(n_x)):
                for k in reversed(range(2)):
                    n = ((i * n_a + p) * n_x + u) * 2 + k
                    if n:
                        dev = (ups[p] * 2 + (1 - b if i else b), xs[u] * 2 + (1 - c if k else c))
                        row = sv.at[i * n_a + near_slot[p]]
                        send(row, sd.at[((i * n_a + far_slot[p]) * n_x + (n_x - u) % n_x) * 2 + k], dev, sums)
    sd[0] = part
    send(sq.at[0], sq.at[1], sib, squashed)
    embed.own_across()
    embed.spread(others[2:])
    arrived(facts)
    for i in range(2):
        for j in range(n_a):
            k = i * n_a + j
            for f in range(3):
                ids[f:f + 1, k * rows:(k + 1) * rows] = ma[i, j, :, f * rows:(f + 1) * rows]
    base = (d * n_t + t) * vocab
    column = (base + lax.broadcasted_iota(jnp.int32, (vocab, tokens), 0)).astype(f32)
    lhs[:, tokens:] = jnp.where(column == ids[1:2, :], 1.0, 0.0).astype(bf16)
    embed.cross()
    arrived(squashed)
    arrived(shared)
    arrived(sums)
    total = jnp.sum(sd[...], axis=0)
    shift = ((1 - 2 * c) * vocab).astype(f32)
    for k in range(2):
        squash = sq[k]
        hits = jnp.where(column == ids[0:1, :] - k * shift, 1.0, 0.0)
        dlogit = ids[2:3, :] * (jnp.exp(30.0 * squash) / total - hits) * (1.0 - squash * squash)
        if k == 0:
            lhs[:, :tokens] = dlogit.astype(bf16)
        dlt[k] = jnp.transpose(dlogit).astype(bf16)

    cut = min((cols // 128 + 1) // 2 * 128, cols) if aligned else cols
    split = cut < cols
    back = tokens // 2

    def pair(mine, theirs):
        return jnp.dot(dlt[0], mine, preferred_element_type=f32) + jnp.dot(dlt[1], theirs, preferred_element_type=f32)

    def term(u, start, stop):
        if aligned:
            at = lanes((2 * xs[u] + c) * cols + start, stop - start)
            return pair(tab[:, at], tabs[xs[u], :, start:stop])
        wide = jnp.zeros((tokens, cols), f32)
        for n in range(n_t):
            at = slice(n * cols, (n + 1) * cols)
            wide = jnp.where(2 * xs[u] + c == n, pair(tab[:, at], tabs[0, :, at]), wide)
        return wide

    order = list(range(1, n_x)) + [0]
    xa1, xa0, yb1, yb0, y2a, x2b, z3a, z3b = [group() for n in range(8)]
    for u in order[:-1]:
        qa[u] = term(u, 0, cut).astype(bf16)
        for low_row, g in ((back, xa1), (0, xa0)):
            at = slice(low_row, low_row + back)
            send(qa.at[u, at], ra.at[n_x - u, at], (d, xs[u] * 2 + c), g)
    if split:
        for u in order:
            value = term(u, cut, cols)
            qb[u] = value[back:].astype(bf16)
            send(qb.at[u], rb.at[u], side, yb1 if u else yb0)
            pf[u, :back, cut:] = value[:back]
    pf[0, :, :cut] = term(0, 0, cut)
    embed.close()
    step = 256 if width % 256 == 0 else 128

    def table_cols(start, stop):
        for i in range(start, stop):
            at = slice(i * step, (i + 1) * step)
            both = gb[:, :, :, :, at].reshape(2 * tokens, step)
            head = jnp.dot(lhs[:, :tokens], both[:tokens], preferred_element_type=f32)
            tail = jnp.dot(lhs[:, tokens:], both[tokens:], preferred_element_type=f32)
            tg[:, at] = (head + scale * tail).astype(bf16)

    def over_x(at):
        value = pf[0, at, :cut]
        for u in range(1, n_x):
            value = value + ra[u, at].astype(f32)
        return value

    def over_side(u):
        return pf[u, :back, cut:] + rb[u].astype(f32)

    arrived(xa1)
    q2a[...] = over_x(slice(back, tokens)).astype(bf16)
    send(q2a, r2a, side, y2a)
    if split:
        arrived(yb1)
        for u in range(1, n_x):
            q2b[u] = over_side(u).astype(bf16)
            send(q2b.at[u], r2b.at[n_x - u], (d, xs[u] * 2 + c), x2b)
    arrived(xa0)
    acc[:, :cut] = over_x(slice(0, back))
    if split:
        arrived(yb0)
        acc[:, cut:] = over_side(0)
    arrived(embed.s0)
    arrived(embed.s1)
    tiles = width // step
    early = tiles // 2
    table_cols(0, early)
    arrived(y2a)
    acc[:, :cut] = acc[:, :cut] + r2a[...].astype(f32)
    for p in reversed(others):
        k = pl.multiple_of(near_slot[p] * rows, rows)
        q3a[p] = acc[pl.ds(k, rows), :cut].astype(bf16)
        send(q3a.at[p], r3a.at[far_slot[p]], (ups[p] * 2 + b, t), z3a)
    if split:
        arrived(x2b)
        value = acc[:, cut:]
        for u in range(1, n_x):
            value = value + r2b[u].astype(f32)
        acc[:, cut:] = value
        for p in reversed(others):
            k = pl.multiple_of(near_slot[p] * rows, rows)
            q3b[p] = acc[pl.ds(k, rows), cut:].astype(bf16)
            send(q3b.at[p], r3b.at[far_slot[p]], (ups[p] * 2 + b, t), z3b)
    table_cols(early, tiles)
    arrived(z3a)
    out = acc[:rows, :cut]
    for j in others:
        out = out + r3a[j].astype(f32)
    hg[:, :cut] = out
    if split:
        arrived(z3b)
        out = acc[:rows, cut:]
        for j in others:
            out = out + r3b[j].astype(f32)
        hg[:, cut:] = out
    whole(total_sent[0], 0).wait_send()


def write(tg, hg, tg_out, hg_out, sems):
    copies = [pltpu.make_async_copy(tg, tg_out, sems.at[0]), pltpu.make_async_copy(hg, hg_out, sems.at[1])]
    for copy in copies:
        copy.start()
    for copy in copies:
        copy.wait()


def per_device(n_dp, n_t, hidden, tied_table, targets, loss_weight, inputs, embed_grad):
    rows, width = hidden.shape
    vocab = tied_table.shape[0]
    tokens, cols, n_x, n_a = n_dp * rows, width // n_t, n_t // 2, n_dp // 2
    f32, bf16 = jnp.float32, jnp.bfloat16
    vmem, hbm = pl.BlockSpec(memory_space=pltpu.VMEM), pl.BlockSpec(memory_space=pl.ANY)
    cut = min((cols // 128 + 1) // 2 * 128, cols) if cols % 128 == 0 else cols
    rest = cols - cut or 128
    receives = 2 * (3 * n_a + 5) + 4 + 8
    grads = pl.pallas_call(
        functools.partial(kernel, n_dp, n_t, math.sqrt(width)),
        out_shape=(
            pltpu.VMEM((vocab, width), bf16),
            pltpu.VMEM((rows, cols), f32),
        ),
        in_specs=[hbm] * 6,
        out_specs=(vmem, vmem),
        scratch_shapes=[
            pltpu.VMEM((1, rows), jnp.int32),
            pltpu.VMEM((1, rows), jnp.int32),
            pltpu.VMEM((1, rows), bf16),
            pltpu.VMEM((2, 2, n_a, rows, width), bf16),
            pltpu.VMEM((2, n_a, 1, 128), f32),
            pltpu.VMEM((8, tokens), f32),
            pltpu.VMEM((vocab, width), bf16),
            pltpu.VMEM((n_x, vocab, cols) if cols % 128 == 0 else (1, vocab, width), bf16),
            pltpu.VMEM((2, vocab, tokens), f32),
            pltpu.VMEM((vocab, 2 * tokens), bf16),
            pltpu.VMEM((2, tokens, vocab), bf16),
            pltpu.VMEM((n_dp, 1, tokens), f32),
            pltpu.VMEM((n_dp * n_t, 1, tokens), f32),
            pltpu.VMEM((n_x, tokens, cols), f32),
            pltpu.VMEM((n_x, tokens, cut), bf16),
            pltpu.VMEM((n_x, tokens, cut), bf16),
            pltpu.VMEM((n_x, tokens // 2, rest), bf16),
            pltpu.VMEM((n_x, tokens // 2, rest), bf16),
            pltpu.VMEM((tokens // 2, cut), bf16),
            pltpu.VMEM((tokens // 2, cut), bf16),
            pltpu.VMEM((n_x, tokens // 2, rest), bf16),
            pltpu.VMEM((n_x, tokens // 2, rest), bf16),
            pltpu.VMEM((tokens // 2, cols), f32),
            pltpu.VMEM((n_a, rows, cut), bf16),
            pltpu.VMEM((n_a, rows, cut), bf16),
            pltpu.VMEM((n_a, rows, rest), bf16),
            pltpu.VMEM((n_a, rows, rest), bf16),
            pltpu.VMEM((tokens * width // 32, 1, 128), f32),
            pltpu.SemaphoreType.DMA((1,)),
            pltpu.SemaphoreType.DMA((receives,)),
            pltpu.SemaphoreType.DMA((6,)),
        ],
        compiler_params=pltpu.CompilerParams(
            collective_id=0, has_side_effects=True, vmem_limit_bytes=56 << 20
        ),
    )(targets[None], inputs[None], loss_weight[None], hidden, embed_grad, tied_table)
    return pl.pallas_call(
        write,
        out_shape=(jax.ShapeDtypeStruct((vocab, width), bf16), jax.ShapeDtypeStruct((rows, cols), f32)),
        in_specs=[vmem] * 2,
        out_specs=(hbm, hbm),
        scratch_shapes=[pltpu.SemaphoreType.DMA((2,))],
        compiler_params=pltpu.CompilerParams(vmem_limit_bytes=1 << 20),
    )(*grads)


def solution(mesh):
    placed = (P("dp", None), P(("dp", "tensor"), None), P("dp"), P("dp"), P("dp"), P("dp", None))
    return jax.shard_map(
        functools.partial(per_device, mesh.shape["dp"], mesh.shape["tensor"]),
        mesh=mesh,
        in_specs=placed,
        out_specs=(P(("dp", "tensor"), None), P("dp", "tensor")),
        check_vma=False,
    )
```

```python
import functools
import math

import jax
import jax.numpy as jnp
from jax import lax
from jax.experimental import pallas as pl
from jax.experimental.pallas import tpu as pltpu
from jax.sharding import PartitionSpec as P

MESH = pl.DeviceIdType.MESH
LANES = (((1,), (1,)), ((), ()))


def kernel(
    n_dp, n_t, scale,
    targets, inputs, weights, hid, emb, table, tg, hg,
    tgt, inp, wts, gb, ma, ids, tab, tabs, sq, lhs, dlt, sv, sd, pf, qa, ra, qb, rb, q2a, r2a, q2b, r2b,
    q3a, r3a, q3b, r3b, span, ss, rs, ls,
):
    d, t = lax.axis_index("dp"), lax.axis_index("tensor")
    n_a, n_x = n_dp // 2, n_t // 2
    a, b = lax.div(d, 2), lax.rem(d, 2)
    x, c = lax.div(t, 2), lax.rem(t, 2)
    e = lax.rem(x, 2)
    rows, width = hid.shape
    tokens = n_dp * rows
    vocab = tab.shape[0]
    half, quarter, cols = width // 2, width // 4, width // n_t
    f32, bf16 = jnp.float32, jnp.bfloat16
    hb, eb = gb.at[0], gb.at[1]
    others = range(1, n_a)
    low = a < n_a // 2

    xs = [x] + [lax.rem(x + j, n_x) for j in range(1, n_x)]
    side, sib, across = (a * 2 + 1 - b, t), (d, x * 2 + 1 - c), (d, (x + 1 - 2 * e) * 2 + c)
    near_slot = [0] + [jnp.where(low, p, n_a - p) for p in others]
    far_slot = [0] + [jnp.where(low, n_a - p, p) for p in others]
    ups = [a] + [lax.rem(a + near_slot[p], n_a) for p in others]

    barrier = pltpu.get_barrier_semaphore()
    greet = [(ups[p] * 2 + b, t) for p in others] + [side, across, sib]
    for u in range(2, n_x):
        pair = lax.rem(x - e + u, n_x)
        for dp in range(n_dp):
            for k in range(2):
                if u % 2 == 0:
                    greet += [(dp, (pair + i) * 2 + k) for i in range(2)]
    for dev in greet:
        pl.semaphore_signal(barrier, inc=1, device_id=dev, device_id_type=MESH)

    loads = [
        pltpu.make_async_copy(hid, hb.at[0, 0], ls.at[0]),
        pltpu.make_async_copy(emb, eb.at[0, 0], ls.at[1]),
        pltpu.make_async_copy(table, tab, ls.at[2]),
        pltpu.make_async_copy(targets, tgt, ls.at[3]),
        pltpu.make_async_copy(inputs, inp, ls.at[4]),
        pltpu.make_async_copy(weights, wts, ls.at[5]),
    ]
    for n in (0, 3, 4, 5, 1, 2):
        loads[n].start()

    groups, total_sent = [], [0]

    def group(size=1):
        groups.append([0, size, sum(g[1] for g in groups)])
        return groups[-1]

    def send(src, dst, dev, g, at=0):
        size = math.prod(src.shape) * src.dtype.itemsize
        g[0] += size
        total_sent[0] += size
        pltpu.make_async_remote_copy(
            src_ref=src, dst_ref=dst, send_sem=ss.at[0], recv_sem=rs.at[g[2] + at], device_id=dev, device_id_type=MESH
        ).start()

    def whole(size, at):
        ref = span.at[pl.ds(0, size // 512)]
        return pltpu.make_async_remote_copy(
            src_ref=ref, dst_ref=ref, send_sem=ss.at[0], recv_sem=rs.at[at], device_id=side, device_id_type=MESH
        )

    def arrived(g, at=0, parts=1):
        whole(g[0] // parts, g[2] + at).wait_recv()

    def lanes(at, size):
        return pl.ds(pl.multiple_of(at, 128), size)

    near = lanes((c * 2 + e) * quarter, quarter)
    far = lanes((c * 2 + 1 - e) * quarter, quarter)
    mine = lanes(c * half, half)
    first = (quarter // 128 + 1) // 2 * 128
    near_a = lanes((c * 2 + e) * quarter, first)
    far_b = lanes((c * 2 + 1 - e) * quarter + first, quarter - first)

    class Gather:
        def __init__(self, buf):
            self.buf = buf
            self.z, self.y, self.x, self.own = group(n_a), group(n_a), group(n_a), group()
            self.own_x, self.both, self.s0, self.s1 = group(), group(), group(), group()

        def start(self):
            buf = self.buf
            for p in reversed(others):
                k = far_slot[p]
                send(buf.at[0, 0, :, near], buf.at[0, k, :, near], (ups[p] * 2 + b, t), self.z, k)

        def own_side(self):
            send(self.buf.at[0, 0, :, near], self.buf.at[1, 0, :, near], side, self.own)

        def spread(self, which):
            buf = self.buf
            for p in which:
                k = near_slot[p]
                arrived(self.z, k, n_a - 1)
                send(buf.at[0, k, :, near], buf.at[0, k, :, near], across, self.x, p)
                send(buf.at[0, k, :, near], buf.at[1, k, :, near], side, self.y, p)

        def own_across(self):
            buf = self.buf
            arrived(self.own)
            send(buf.at[1, 0, :, near], buf.at[1, 0, :, near], across, self.both)

        def cross(self):
            buf = self.buf
            for p in others:
                k = near_slot[p]
                arrived(self.x, p, n_a - 1)
                send(buf.at[0, k, :, far_b], buf.at[1, k, :, far_b], side, self.both)
                arrived(self.y, p, n_a - 1)
                send(buf.at[1, k, :, near_a], buf.at[1, k, :, near_a], across, self.both)

        def share(self):
            buf = self.buf
            send(buf.at[0, 1:n_a, :, mine], buf.at[0, 1:n_a, :, mine], sib, self.s0)
            send(buf.at[1, :, :, near], buf.at[1, :, :, near], sib, self.s0)

        def close(self):
            buf = self.buf
            arrived(self.both)
            send(buf.at[1, :, :, far], buf.at[1, :, :, far], sib, self.s1)

    hidden, embed = Gather(hb), Gather(eb)
    pl.semaphore_wait(barrier, len(greet))
    loads[0].wait()
    hidden.start()
    hidden.own_side()
    aligned = cols % 128 == 0
    shared, squashed = group(), group()
    if aligned:
        for u in range(n_x):
            send(table.at[:, lanes((2 * u + 1 - c) * cols, cols)], tabs.at[u], sib, shared)
    else:
        send(table, tabs.at[0], sib, shared)
    for n in (3, 4, 5):
        loads[n].wait()
    ma[0, 0] = jnp.zeros(ma.shape[2:], f32)
    ma[0, 0, :, 0:rows] = tgt[...].astype(f32)
    ma[0, 0, :, rows:2 * rows] = inp[...].astype(f32)
    ma[0, 0, :, 2 * rows:3 * rows] = wts[...].astype(f32)
    hidden.spread(others)
    hidden.own_across()
    loads[1].wait()
    embed.start()
    hidden.cross()
    hidden.share()
    facts = group()
    for i in range(2):
        for p in reversed(range(n_a)):
            if i + p:
                dev = (ups[p] * 2 + (1 - b if i else b), t)
                send(ma.at[0, 0], ma.at[i, far_slot[p]], dev, facts)
    loads[2].wait()
    piece = min(vocab, 256)

    def product(i, part, core):
        at = pl.ds(i * piece, piece)
        part_lanes = lanes((core * 2 + part) * quarter, quarter)
        return at, lax.dot_general(
            tab[at, part_lanes], hb[:, :, :, part_lanes].reshape(tokens, quarter), LANES, preferred_element_type=f32
        )

    def quarters(part, core, fresh=False):
        for i in range(vocab // piece):
            at, value = product(i, part, core)
            sq[0, at, :] = value if fresh else sq[0, at, :] + value

    def last(i, total):
        at, value = product(i, 1 - e, 1 - c)
        squash = jnp.tanh((sq[0, at, :] + value) / 30.0)
        sq[0, at, :] = squash
        return total + jnp.sum(jnp.exp(30.0 * squash), axis=0, keepdims=True)

    quarters(e, c, True)
    hidden.close()
    embed.own_side()
    embed.spread(others[:2])
    quarters(1 - e, c)
    arrived(hidden.s0)
    quarters(e, 1 - c)
    arrived(hidden.s1)
    part = jnp.zeros((1, tokens), f32)
    for i in range(vocab // piece):
        part = last(i, part)

    lane = lax.rem(lax.broadcasted_iota(jnp.int32, (1, tokens), 1), tokens // 2)
    for i in range(2):
        for j in range(n_a):
            move = j * rows
            value = part
            if i:
                value = pltpu.roll(value, tokens // 2, 1)
            if j:
                value = jnp.where(
                    lane < tokens // 2 - move,
                    pltpu.roll(value, tokens - move, 1),
                    pltpu.roll(value, tokens // 2 - move, 1),
                )
            sv[i * n_a + j] = value
    sums = group()
    for p in reversed(range(n_a)):
        for i in reversed(range(2)):
            for u in reversed(range(n_x)):
                for k in reversed(range(2)):
                    n = ((i * n_a + p) * n_x + u) * 2 + k
                    if n:
                        dev = (ups[p] * 2 + (1 - b if i else b), xs[u] * 2 + (1 - c if k else c))
                        row = sv.at[i * n_a + near_slot[p]]
                        send(row, sd.at[((i * n_a + far_slot[p]) * n_x + (n_x - u) % n_x) * 2 + k], dev, sums)
    sd[0] = part
    send(sq.at[0], sq.at[1], sib, squashed)
    embed.own_across()
    embed.spread(others[2:])
    arrived(facts)
    for i in range(2):
        for j in range(n_a):
            k = i * n_a + j
            for f in range(3):
                ids[f:f + 1, k * rows:(k + 1) * rows] = ma[i, j, :, f * rows:(f + 1) * rows]
    base = (d * n_t + t) * vocab
    column = (base + lax.broadcasted_iota(jnp.int32, (vocab, tokens), 0)).astype(f32)
    lhs[:, tokens:] = jnp.where(column == ids[1:2, :], 1.0, 0.0).astype(bf16)
    embed.cross()
    embed.share()
    arrived(squashed)
    arrived(shared)
    arrived(sums)
    total = jnp.sum(sd[...], axis=0)
    shift = ((1 - 2 * c) * vocab).astype(f32)
    for k in range(2):
        squash = sq[k]
        hits = jnp.where(column == ids[0:1, :] - k * shift, 1.0, 0.0)
        dlogit = ids[2:3, :] * (jnp.exp(30.0 * squash) / total - hits) * (1.0 - squash * squash)
        if k == 0:
            lhs[:, :tokens] = dlogit.astype(bf16)
        dlt[k] = jnp.transpose(dlogit).astype(bf16)

    cut = min((cols // 128 + 1) // 2 * 128, cols) if aligned else cols
    split = cut < cols
    back = tokens // 2

    def pair(mine, theirs):
        return jnp.dot(dlt[0], mine, preferred_element_type=f32) + jnp.dot(dlt[1], theirs, preferred_element_type=f32)

    def term(u, start, stop):
        if aligned:
            at = lanes((2 * xs[u] + c) * cols + start, stop - start)
            return pair(tab[:, at], tabs[xs[u], :, start:stop])
        wide = jnp.zeros((tokens, cols), f32)
        for n in range(n_t):
            at = slice(n * cols, (n + 1) * cols)
            wide = jnp.where(2 * xs[u] + c == n, pair(tab[:, at], tabs[0, :, at]), wide)
        return wide

    order = list(range(1, n_x)) + [0]
    steps = list(reversed(range(n_a)))
    xa1, xa0, yb1, y2a, x2b = [[group() for p in range(n_a)] for n in range(5)]
    yb0, z3 = group(), group()

    def block(p, i=0):
        return pl.ds(i * back + pl.multiple_of(near_slot[p] * rows, rows) if p else i * back, rows)

    def send_x(p, i, g):
        for u in order[:-1]:
            at = block(p, i)
            send(qa.at[u, at], ra.at[n_x - u, at], (d, xs[u] * 2 + c), g)

    for u in order[:-1]:
        qa[u] = term(u, 0, cut).astype(bf16)
    for p in steps:
        send_x(p, 1, xa1[p])
    for u in order:
        if split:
            value = term(u, cut, cols)
            qb[u] = value[back:].astype(bf16)
            pf[u, :back, cut:] = value[:back]
        if split and u == order[-2]:
            for p in steps:
                for v in order[:-1]:
                    send(qb.at[v, block(p)], rb.at[v, block(p)], side, yb1[p])
    for p in steps[:2]:
        send_x(p, 0, xa0[p])
    if split:
        send(qb.at[0], rb.at[0], side, yb0)
    pf[0, :, :cut] = term(0, 0, cut)
    step = 256 if width % 256 == 0 else 128

    def table_cols(start, stop):
        for i in range(start, stop):
            at = slice(i * step, (i + 1) * step)
            both = gb[:, :, :, :, at].reshape(2 * tokens, step)
            head = jnp.dot(lhs[:, :tokens], both[:tokens], preferred_element_type=f32)
            tail = jnp.dot(lhs[:, tokens:], both[tokens:], preferred_element_type=f32)
            tg[:, at] = (head + scale * tail).astype(bf16)

    def over_x(p, i):
        at = block(p, i)
        value = pf[0, at, :cut]
        for u in range(1, n_x):
            value = value + ra[u, at].astype(f32)
        return value

    for n, p in enumerate(steps):
        at = block(p)
        arrived(xa1[p])
        q2a[at] = over_x(p, 1).astype(bf16)
        send(q2a.at[at], r2a.at[at], side, y2a[p])
        if split:
            arrived(yb1[p])
            for u in order[:-1]:
                q2b[u, at] = (pf[u, at, cut:] + rb[u, at].astype(f32)).astype(bf16)
                send(q2b.at[u, at], r2b.at[n_x - u, at], (d, xs[u] * 2 + c), x2b[p])
        if n + 2 < n_a:
            send_x(steps[n + 2], 0, xa0[steps[n + 2]])
    embed.close()
    tiles = width // step
    if split:
        arrived(yb0)
    for p in steps:
        at = block(p)
        arrived(xa0[p])
        value = over_x(p, 0)
        arrived(y2a[p])
        value = value + r2a[at].astype(f32)
        if p:
            q3a[p] = value.astype(bf16)
            send(q3a.at[p], r3a.at[far_slot[p]], (ups[p] * 2 + b, t), z3)
        else:
            hg[:, :cut] = value
        if split:
            value = pf[0, at, cut:] + rb[0, at].astype(f32)
            arrived(x2b[p])
            for u in range(1, n_x):
                value = value + r2b[u, at].astype(f32)
            if p:
                q3b[p] = value.astype(bf16)
                send(q3b.at[p], r3b.at[far_slot[p]], (ups[p] * 2 + b, t), z3)
            else:
                hg[:, cut:] = value
    arrived(embed.s0)
    arrived(embed.s1)
    table_cols(0, tiles)
    arrived(z3)
    value = hg[:, :cut]
    for j in others:
        value = value + r3a[j].astype(f32)
    hg[:, :cut] = value
    if split:
        value = hg[:, cut:]
        for j in others:
            value = value + r3b[j].astype(f32)
        hg[:, cut:] = value
    whole(total_sent[0], 0).wait_send()


def write(tg, hg, tg_out, hg_out, sems):
    copies = [pltpu.make_async_copy(tg, tg_out, sems.at[0]), pltpu.make_async_copy(hg, hg_out, sems.at[1])]
    for copy in copies:
        copy.start()
    for copy in copies:
        copy.wait()


def per_device(n_dp, n_t, hidden, tied_table, targets, loss_weight, inputs, embed_grad):
    rows, width = hidden.shape
    vocab = tied_table.shape[0]
    tokens, cols, n_x, n_a = n_dp * rows, width // n_t, n_t // 2, n_dp // 2
    f32, bf16 = jnp.float32, jnp.bfloat16
    vmem, hbm = pl.BlockSpec(memory_space=pltpu.VMEM), pl.BlockSpec(memory_space=pl.ANY)
    cut = min((cols // 128 + 1) // 2 * 128, cols) if cols % 128 == 0 else cols
    rest = cols - cut or 128
    receives = 2 * (3 * n_a + 5) + 4 + 5 * n_a + 2
    grads = pl.pallas_call(
        functools.partial(kernel, n_dp, n_t, math.sqrt(width)),
        out_shape=(
            pltpu.VMEM((vocab, width), bf16),
            pltpu.VMEM((rows, cols), f32),
        ),
        in_specs=[hbm] * 6,
        out_specs=(vmem, vmem),
        scratch_shapes=[
            pltpu.VMEM((1, rows), jnp.int32),
            pltpu.VMEM((1, rows), jnp.int32),
            pltpu.VMEM((1, rows), bf16),
            pltpu.VMEM((2, 2, n_a, rows, width), bf16),
            pltpu.VMEM((2, n_a, 1, 128), f32),
            pltpu.VMEM((8, tokens), f32),
            pltpu.VMEM((vocab, width), bf16),
            pltpu.VMEM((n_x, vocab, cols) if cols % 128 == 0 else (1, vocab, width), bf16),
            pltpu.VMEM((2, vocab, tokens), f32),
            pltpu.VMEM((vocab, 2 * tokens), bf16),
            pltpu.VMEM((2, tokens, vocab), bf16),
            pltpu.VMEM((n_dp, 1, tokens), f32),
            pltpu.VMEM((n_dp * n_t, 1, tokens), f32),
            pltpu.VMEM((n_x, tokens, cols), f32),
            pltpu.VMEM((n_x, tokens, cut), bf16),
            pltpu.VMEM((n_x, tokens, cut), bf16),
            pltpu.VMEM((n_x, tokens // 2, rest), bf16),
            pltpu.VMEM((n_x, tokens // 2, rest), bf16),
            pltpu.VMEM((tokens // 2, cut), bf16),
            pltpu.VMEM((tokens // 2, cut), bf16),
            pltpu.VMEM((n_x, tokens // 2, rest), bf16),
            pltpu.VMEM((n_x, tokens // 2, rest), bf16),
            pltpu.VMEM((n_a, rows, cut), bf16),
            pltpu.VMEM((n_a, rows, cut), bf16),
            pltpu.VMEM((n_a, rows, rest), bf16),
            pltpu.VMEM((n_a, rows, rest), bf16),
            pltpu.VMEM((tokens * width // 32, 1, 128), f32),
            pltpu.SemaphoreType.DMA((1,)),
            pltpu.SemaphoreType.DMA((receives,)),
            pltpu.SemaphoreType.DMA((6,)),
        ],
        compiler_params=pltpu.CompilerParams(
            collective_id=0, has_side_effects=True, vmem_limit_bytes=56 << 20
        ),
    )(targets[None], inputs[None], loss_weight[None], hidden, embed_grad, tied_table)
    return pl.pallas_call(
        write,
        out_shape=(jax.ShapeDtypeStruct((vocab, width), bf16), jax.ShapeDtypeStruct((rows, cols), f32)),
        in_specs=[vmem] * 2,
        out_specs=(hbm, hbm),
        scratch_shapes=[pltpu.SemaphoreType.DMA((2,))],
        compiler_params=pltpu.CompilerParams(vmem_limit_bytes=1 << 20),
    )(*grads)


def solution(mesh):
    placed = (P("dp", None), P(("dp", "tensor"), None), P("dp"), P("dp"), P("dp"), P("dp", None))
    return jax.shard_map(
        functools.partial(per_device, mesh.shape["dp"], mesh.shape["tensor"]),
        mesh=mesh,
        in_specs=placed,
        out_specs=(P(("dp", "tensor"), None), P("dp", "tensor")),
        check_vma=False,
    )
```

```python
import functools
import math

import jax
import jax.numpy as jnp
from jax import lax
from jax.experimental import pallas as pl
from jax.experimental.pallas import tpu as pltpu
from jax.sharding import PartitionSpec as P

MESH = pl.DeviceIdType.MESH
LANES = (((1,), (1,)), ((), ()))


def kernel(
    n_dp, n_t, scale,
    targets, inputs, weights, hid, emb, table, tg, hg,
    tgt, inp, wts, gb, ma, ids, tab, tabs, sq, lhs, dlt, sv, sd, pf, qa, ra, qb, rb, q2a, r2a, q2b, r2b,
    q3a, r3a, q3b, r3b, span, ss, rs, ls,
):
    d, t = lax.axis_index("dp"), lax.axis_index("tensor")
    n_a, n_x = n_dp // 2, n_t // 2
    a, b = lax.div(d, 2), lax.rem(d, 2)
    x, c = lax.div(t, 2), lax.rem(t, 2)
    e = lax.rem(x, 2)
    rows, width = hid.shape
    tokens = n_dp * rows
    vocab = tab.shape[0]
    half, quarter, cols = width // 2, width // 4, width // n_t
    f32, bf16 = jnp.float32, jnp.bfloat16
    hb, eb = gb.at[0], gb.at[1]
    others = range(1, n_a)
    low = a < n_a // 2

    xs = [x] + [lax.rem(x + j, n_x) for j in range(1, n_x)]
    side, sib, across = (a * 2 + 1 - b, t), (d, x * 2 + 1 - c), (d, (x + 1 - 2 * e) * 2 + c)
    near_slot = [0] + [jnp.where(low, p, n_a - p) for p in others]
    far_slot = [0] + [jnp.where(low, n_a - p, p) for p in others]
    ups = [a] + [lax.rem(a + near_slot[p], n_a) for p in others]

    barrier = pltpu.get_barrier_semaphore()
    diag = (side[0], across[1])
    greet = [(ups[p] * 2 + b, t) for p in others] + [side, across, sib, diag]
    for u in range(2, n_x):
        pair = lax.rem(x - e + u, n_x)
        for dp in range(n_dp):
            for k in range(2):
                if u % 2 == 0:
                    greet += [(dp, (pair + i) * 2 + k) for i in range(2)]
    for dev in greet:
        pl.semaphore_signal(barrier, inc=1, device_id=dev, device_id_type=MESH)

    loads = [
        pltpu.make_async_copy(hid, hb.at[0, 0], ls.at[0]),
        pltpu.make_async_copy(emb, eb.at[0, 0], ls.at[1]),
        pltpu.make_async_copy(table, tab, ls.at[2]),
        pltpu.make_async_copy(targets, tgt, ls.at[3]),
        pltpu.make_async_copy(inputs, inp, ls.at[4]),
        pltpu.make_async_copy(weights, wts, ls.at[5]),
    ]
    for n in (0, 3, 4, 5, 1, 2):
        loads[n].start()

    groups, total_sent = [], [0]

    def group(size=1):
        groups.append([0, size, sum(g[1] for g in groups)])
        return groups[-1]

    def send(src, dst, dev, g, at=0):
        size = math.prod(src.shape) * src.dtype.itemsize
        g[0] += size
        total_sent[0] += size
        pltpu.make_async_remote_copy(
            src_ref=src, dst_ref=dst, send_sem=ss.at[0], recv_sem=rs.at[g[2] + at], device_id=dev, device_id_type=MESH
        ).start()

    def whole(size, at):
        ref = span.at[pl.ds(0, size // 512)]
        return pltpu.make_async_remote_copy(
            src_ref=ref, dst_ref=ref, send_sem=ss.at[0], recv_sem=rs.at[at], device_id=side, device_id_type=MESH
        )

    def arrived(g, at=0, parts=1):
        whole(g[0] // parts, g[2] + at).wait_recv()

    def lanes(at, size):
        return pl.ds(pl.multiple_of(at, 128), size)

    near = lanes((c * 2 + e) * quarter, quarter)
    far = lanes((c * 2 + 1 - e) * quarter, quarter)
    mine = lanes(c * half, half)
    first = (quarter // 128 + 1) // 2 * 128
    near_a = lanes((c * 2 + e) * quarter, first)
    far_b = lanes((c * 2 + 1 - e) * quarter + first, quarter - first)

    class Gather:
        def __init__(self, buf, direct):
            self.buf = buf
            self.direct = direct
            self.z, self.y, self.x, self.own = group(n_a), group(n_a), group(n_a), group()
            self.own_x, self.both, self.s0, self.s1 = group(), group(), group(), group()

        def start(self):
            buf = self.buf
            for p in reversed(others):
                k = far_slot[p]
                send(buf.at[0, 0, :, near], buf.at[0, k, :, near], (ups[p] * 2 + b, t), self.z, k)

        def own_side(self):
            send(self.buf.at[0, 0, :, near], self.buf.at[1, 0, :, near], side, self.own)

        def spread(self, which):
            buf = self.buf
            for p in which:
                k = near_slot[p]
                arrived(self.z, k, n_a - 1)
                send(buf.at[0, k, :, near], buf.at[0, k, :, near], across, self.x, p)
                send(buf.at[0, k, :, near], buf.at[1, k, :, near], side, self.y, p)
                if p in self.direct:
                    send(buf.at[0, k, :, near], buf.at[1, k, :, near], diag, self.both)

        def own_across(self):
            buf = self.buf
            arrived(self.own)
            send(buf.at[1, 0, :, near], buf.at[1, 0, :, near], across, self.both)

        def cross(self):
            buf = self.buf
            for p in others:
                k = near_slot[p]
                arrived(self.x, p, n_a - 1)
                if p not in self.direct:
                    send(buf.at[0, k, :, far_b], buf.at[1, k, :, far_b], side, self.both)
                arrived(self.y, p, n_a - 1)
                if p not in self.direct:
                    send(buf.at[1, k, :, near_a], buf.at[1, k, :, near_a], across, self.both)

        def share(self):
            buf = self.buf
            send(buf.at[0, 1:n_a, :, mine], buf.at[0, 1:n_a, :, mine], sib, self.s0)
            send(buf.at[1, :, :, near], buf.at[1, :, :, near], sib, self.s0)

        def close(self):
            buf = self.buf
            arrived(self.both)
            send(buf.at[1, :, :, far], buf.at[1, :, :, far], sib, self.s1)

    hidden, embed = Gather(hb, range(n_a // 2, n_a)), Gather(eb, ())
    pl.semaphore_wait(barrier, len(greet))
    loads[0].wait()
    hidden.start()
    hidden.own_side()
    aligned = cols % 128 == 0
    shared, squashed = group(), group()
    if aligned:
        for u in range(n_x):
            send(table.at[:, lanes((2 * u + 1 - c) * cols, cols)], tabs.at[u], sib, shared)
    else:
        send(table, tabs.at[0], sib, shared)
    for n in (3, 4, 5):
        loads[n].wait()
    ma[0, 0] = jnp.zeros(ma.shape[2:], f32)
    ma[0, 0, :, 0:rows] = tgt[...].astype(f32)
    ma[0, 0, :, rows:2 * rows] = inp[...].astype(f32)
    ma[0, 0, :, 2 * rows:3 * rows] = wts[...].astype(f32)
    hidden.spread(others)
    hidden.own_across()
    loads[1].wait()
    embed.start()
    hidden.cross()
    hidden.share()
    facts = group()
    for i in range(2):
        for p in reversed(range(n_a)):
            if i + p:
                dev = (ups[p] * 2 + (1 - b if i else b), t)
                send(ma.at[0, 0], ma.at[i, far_slot[p]], dev, facts)
    loads[2].wait()
    piece = min(vocab, 256)

    def product(i, part, core):
        at = pl.ds(i * piece, piece)
        part_lanes = lanes((core * 2 + part) * quarter, quarter)
        return at, lax.dot_general(
            tab[at, part_lanes], hb[:, :, :, part_lanes].reshape(tokens, quarter), LANES, preferred_element_type=f32
        )

    def quarters(part, core, fresh=False):
        for i in range(vocab // piece):
            at, value = product(i, part, core)
            sq[0, at, :] = value if fresh else sq[0, at, :] + value

    def last(i, total):
        at, value = product(i, 1 - e, 1 - c)
        squash = jnp.tanh((sq[0, at, :] + value) / 30.0)
        sq[0, at, :] = squash
        return total + jnp.sum(jnp.exp(30.0 * squash), axis=0, keepdims=True)

    quarters(e, c, True)
    hidden.close()
    embed.own_side()
    embed.spread(others[:2])
    quarters(1 - e, c)
    arrived(hidden.s0)
    quarters(e, 1 - c)
    arrived(hidden.s1)
    part = jnp.zeros((1, tokens), f32)
    for i in range(vocab // piece):
        part = last(i, part)

    lane = lax.rem(lax.broadcasted_iota(jnp.int32, (1, tokens), 1), tokens // 2)
    for i in range(2):
        for j in range(n_a):
            move = j * rows
            value = part
            if i:
                value = pltpu.roll(value, tokens // 2, 1)
            if j:
                value = jnp.where(
                    lane < tokens // 2 - move,
                    pltpu.roll(value, tokens - move, 1),
                    pltpu.roll(value, tokens // 2 - move, 1),
                )
            sv[i * n_a + j] = value
    sums = group()
    for p in reversed(range(n_a)):
        for i in reversed(range(2)):
            for u in reversed(range(n_x)):
                for k in reversed(range(2)):
                    n = ((i * n_a + p) * n_x + u) * 2 + k
                    if n:
                        dev = (ups[p] * 2 + (1 - b if i else b), xs[u] * 2 + (1 - c if k else c))
                        row = sv.at[i * n_a + near_slot[p]]
                        send(row, sd.at[((i * n_a + far_slot[p]) * n_x + (n_x - u) % n_x) * 2 + k], dev, sums)
    sd[0] = part
    send(sq.at[0], sq.at[1], sib, squashed)
    embed.own_across()
    embed.spread(others[2:])
    arrived(facts)
    for i in range(2):
        for j in range(n_a):
            k = i * n_a + j
            for f in range(3):
                ids[f:f + 1, k * rows:(k + 1) * rows] = ma[i, j, :, f * rows:(f + 1) * rows]
    base = (d * n_t + t) * vocab
    column = (base + lax.broadcasted_iota(jnp.int32, (vocab, tokens), 0)).astype(f32)
    lhs[:, tokens:] = jnp.where(column == ids[1:2, :], 1.0, 0.0).astype(bf16)
    embed.cross()
    embed.share()
    arrived(squashed)
    arrived(shared)
    arrived(sums)
    total = jnp.sum(sd[...], axis=0)
    shift = ((1 - 2 * c) * vocab).astype(f32)
    for k in range(2):
        squash = sq[k]
        hits = jnp.where(column == ids[0:1, :] - k * shift, 1.0, 0.0)
        dlogit = ids[2:3, :] * (jnp.exp(30.0 * squash) / total - hits) * (1.0 - squash * squash)
        if k == 0:
            lhs[:, :tokens] = dlogit.astype(bf16)
        dlt[k] = jnp.transpose(dlogit).astype(bf16)

    cut = min((cols // 128 + 1) // 2 * 128, cols) if aligned else cols
    split = cut < cols
    back = tokens // 2

    def pair(mine, theirs):
        return jnp.dot(dlt[0], mine, preferred_element_type=f32) + jnp.dot(dlt[1], theirs, preferred_element_type=f32)

    def term(u, start, stop):
        if aligned:
            at = lanes((2 * xs[u] + c) * cols + start, stop - start)
            return pair(tab[:, at], tabs[xs[u], :, start:stop])
        wide = jnp.zeros((tokens, cols), f32)
        for n in range(n_t):
            at = slice(n * cols, (n + 1) * cols)
            wide = jnp.where(2 * xs[u] + c == n, pair(tab[:, at], tabs[0, :, at]), wide)
        return wide

    order = list(range(1, n_x)) + [0]
    steps = list(reversed(range(n_a)))
    xa1, xa0, yb1, y2a, x2b = [[group() for p in range(n_a)] for n in range(5)]
    yb0, z3 = group(), group()

    def block(p, i=0):
        return pl.ds(i * back + pl.multiple_of(near_slot[p] * rows, rows) if p else i * back, rows)

    def send_x(p, i, g):
        for u in order[:-1]:
            at = block(p, i)
            send(qa.at[u, at], ra.at[n_x - u, at], (d, xs[u] * 2 + c), g)

    for u in order[:-1]:
        qa[u] = term(u, 0, cut).astype(bf16)
    for p in steps:
        send_x(p, 1, xa1[p])
    for u in order:
        if split:
            value = term(u, cut, cols)
            qb[u] = value[back:].astype(bf16)
            pf[u, :back, cut:] = value[:back]
        if split and u == order[-2]:
            for p in steps:
                for v in order[:-1]:
                    send(qb.at[v, block(p)], rb.at[v, block(p)], side, yb1[p])
    for p in steps[:2]:
        send_x(p, 0, xa0[p])
    if split:
        send(qb.at[0], rb.at[0], side, yb0)
    pf[0, :, :cut] = term(0, 0, cut)
    step = 256 if width % 256 == 0 else 128

    def table_cols(start, stop):
        for i in range(start, stop):
            at = slice(i * step, (i + 1) * step)
            both = gb[:, :, :, :, at].reshape(2 * tokens, step)
            head = jnp.dot(lhs[:, :tokens], both[:tokens], preferred_element_type=f32)
            tail = jnp.dot(lhs[:, tokens:], both[tokens:], preferred_element_type=f32)
            tg[:, at] = (head + scale * tail).astype(bf16)

    def over_x(p, i):
        at = block(p, i)
        value = pf[0, at, :cut]
        for u in range(1, n_x):
            value = value + ra[u, at].astype(f32)
        return value

    for n, p in enumerate(steps):
        at = block(p)
        arrived(xa1[p])
        q2a[at] = over_x(p, 1).astype(bf16)
        send(q2a.at[at], r2a.at[at], side, y2a[p])
        if split:
            arrived(yb1[p])
            for u in order[:-1]:
                q2b[u, at] = (pf[u, at, cut:] + rb[u, at].astype(f32)).astype(bf16)
                send(q2b.at[u, at], r2b.at[n_x - u, at], (d, xs[u] * 2 + c), x2b[p])
        if n + 2 < n_a:
            send_x(steps[n + 2], 0, xa0[steps[n + 2]])
    embed.close()
    tiles = width // step
    if split:
        arrived(yb0)
    for p in steps:
        at = block(p)
        arrived(xa0[p])
        value = over_x(p, 0)
        arrived(y2a[p])
        value = value + r2a[at].astype(f32)
        if p:
            q3a[p] = value.astype(bf16)
            send(q3a.at[p], r3a.at[far_slot[p]], (ups[p] * 2 + b, t), z3)
        else:
            hg[:, :cut] = value
        if split:
            value = pf[0, at, cut:] + rb[0, at].astype(f32)
            arrived(x2b[p])
            for u in range(1, n_x):
                value = value + r2b[u, at].astype(f32)
            if p:
                q3b[p] = value.astype(bf16)
                send(q3b.at[p], r3b.at[far_slot[p]], (ups[p] * 2 + b, t), z3)
            else:
                hg[:, cut:] = value
    arrived(embed.s0)
    arrived(embed.s1)
    table_cols(0, tiles)
    arrived(z3)
    value = hg[:, :cut]
    for j in others:
        value = value + r3a[j].astype(f32)
    hg[:, :cut] = value
    if split:
        value = hg[:, cut:]
        for j in others:
            value = value + r3b[j].astype(f32)
        hg[:, cut:] = value
    whole(total_sent[0], 0).wait_send()


def write(tg, hg, tg_out, hg_out, sems):
    copies = [pltpu.make_async_copy(tg, tg_out, sems.at[0]), pltpu.make_async_copy(hg, hg_out, sems.at[1])]
    for copy in copies:
        copy.start()
    for copy in copies:
        copy.wait()


def per_device(n_dp, n_t, hidden, tied_table, targets, loss_weight, inputs, embed_grad):
    rows, width = hidden.shape
    vocab = tied_table.shape[0]
    tokens, cols, n_x, n_a = n_dp * rows, width // n_t, n_t // 2, n_dp // 2
    f32, bf16 = jnp.float32, jnp.bfloat16
    vmem, hbm = pl.BlockSpec(memory_space=pltpu.VMEM), pl.BlockSpec(memory_space=pl.ANY)
    cut = min((cols // 128 + 1) // 2 * 128, cols) if cols % 128 == 0 else cols
    rest = cols - cut or 128
    receives = 2 * (3 * n_a + 5) + 4 + 5 * n_a + 2
    grads = pl.pallas_call(
        functools.partial(kernel, n_dp, n_t, math.sqrt(width)),
        out_shape=(
            pltpu.VMEM((vocab, width), bf16),
            pltpu.VMEM((rows, cols), f32),
        ),
        in_specs=[hbm] * 6,
        out_specs=(vmem, vmem),
        scratch_shapes=[
            pltpu.VMEM((1, rows), jnp.int32),
            pltpu.VMEM((1, rows), jnp.int32),
            pltpu.VMEM((1, rows), bf16),
            pltpu.VMEM((2, 2, n_a, rows, width), bf16),
            pltpu.VMEM((2, n_a, 1, 128), f32),
            pltpu.VMEM((8, tokens), f32),
            pltpu.VMEM((vocab, width), bf16),
            pltpu.VMEM((n_x, vocab, cols) if cols % 128 == 0 else (1, vocab, width), bf16),
            pltpu.VMEM((2, vocab, tokens), f32),
            pltpu.VMEM((vocab, 2 * tokens), bf16),
            pltpu.VMEM((2, tokens, vocab), bf16),
            pltpu.VMEM((n_dp, 1, tokens), f32),
            pltpu.VMEM((n_dp * n_t, 1, tokens), f32),
            pltpu.VMEM((n_x, tokens, cols), f32),
            pltpu.VMEM((n_x, tokens, cut), bf16),
            pltpu.VMEM((n_x, tokens, cut), bf16),
            pltpu.VMEM((n_x, tokens // 2, rest), bf16),
            pltpu.VMEM((n_x, tokens // 2, rest), bf16),
            pltpu.VMEM((tokens // 2, cut), bf16),
            pltpu.VMEM((tokens // 2, cut), bf16),
            pltpu.VMEM((n_x, tokens // 2, rest), bf16),
            pltpu.VMEM((n_x, tokens // 2, rest), bf16),
            pltpu.VMEM((n_a, rows, cut), bf16),
            pltpu.VMEM((n_a, rows, cut), bf16),
            pltpu.VMEM((n_a, rows, rest), bf16),
            pltpu.VMEM((n_a, rows, rest), bf16),
            pltpu.VMEM((tokens * width // 32, 1, 128), f32),
            pltpu.SemaphoreType.DMA((1,)),
            pltpu.SemaphoreType.DMA((receives,)),
            pltpu.SemaphoreType.DMA((6,)),
        ],
        compiler_params=pltpu.CompilerParams(
            collective_id=0, has_side_effects=True, vmem_limit_bytes=56 << 20
        ),
    )(targets[None], inputs[None], loss_weight[None], hidden, embed_grad, tied_table)
    return pl.pallas_call(
        write,
        out_shape=(jax.ShapeDtypeStruct((vocab, width), bf16), jax.ShapeDtypeStruct((rows, cols), f32)),
        in_specs=[vmem] * 2,
        out_specs=(hbm, hbm),
        scratch_shapes=[pltpu.SemaphoreType.DMA((2,))],
        compiler_params=pltpu.CompilerParams(vmem_limit_bytes=1 << 20),
    )(*grads)


def solution(mesh):
    placed = (P("dp", None), P(("dp", "tensor"), None), P("dp"), P("dp"), P("dp"), P("dp", None))
    return jax.shard_map(
        functools.partial(per_device, mesh.shape["dp"], mesh.shape["tensor"]),
        mesh=mesh,
        in_specs=placed,
        out_specs=(P(("dp", "tensor"), None), P("dp", "tensor")),
        check_vma=False,
    )
```

```python
import functools
import math

import jax
import jax.numpy as jnp
from jax import lax
from jax.experimental import pallas as pl
from jax.experimental.pallas import tpu as pltpu
from jax.sharding import PartitionSpec as P

MESH = pl.DeviceIdType.MESH
LANES = (((1,), (1,)), ((), ()))


def kernel(
    n_dp, n_t, scale,
    targets, inputs, weights, hid, emb, table, tg, hg,
    tgt, inp, wts, gb, ma, ids, tab, tabs, sq, lhs, dlt, sv, sd, pf, qa, ra, qb, rb, q2a, r2a, q2b, r2b,
    q3a, r3a, q3b, r3b, span, ss, rs, ls,
):
    d, t = lax.axis_index("dp"), lax.axis_index("tensor")
    n_a, n_x = n_dp // 2, n_t // 2
    a, b = lax.div(d, 2), lax.rem(d, 2)
    x, c = lax.div(t, 2), lax.rem(t, 2)
    e = lax.rem(x, 2)
    rows, width = hid.shape
    tokens = n_dp * rows
    vocab = tab.shape[0]
    half, quarter, cols = width // 2, width // 4, width // n_t
    f32, bf16 = jnp.float32, jnp.bfloat16
    hb, eb = gb.at[0], gb.at[1]
    others = range(1, n_a)
    low = a < n_a // 2

    xs = [x] + [lax.rem(x + j, n_x) for j in range(1, n_x)]
    side, sib, across = (a * 2 + 1 - b, t), (d, x * 2 + 1 - c), (d, (x + 1 - 2 * e) * 2 + c)
    near_slot = [0] + [jnp.where(low, p, n_a - p) for p in others]
    far_slot = [0] + [jnp.where(low, n_a - p, p) for p in others]
    ups = [a] + [lax.rem(a + near_slot[p], n_a) for p in others]

    barrier = pltpu.get_barrier_semaphore()
    diag = (side[0], across[1])
    greet = [(ups[p] * 2 + b, t) for p in others] + [side, across, sib, diag]
    for u in range(2, n_x):
        pair = lax.rem(x - e + u, n_x)
        for dp in range(n_dp):
            for k in range(2):
                if u % 2 == 0:
                    greet += [(dp, (pair + i) * 2 + k) for i in range(2)]
    for dev in greet:
        pl.semaphore_signal(barrier, inc=1, device_id=dev, device_id_type=MESH)

    loads = [
        pltpu.make_async_copy(hid, hb.at[0, 0], ls.at[0]),
        pltpu.make_async_copy(emb, eb.at[0, 0], ls.at[1]),
        pltpu.make_async_copy(table, tab, ls.at[2]),
        pltpu.make_async_copy(targets, tgt, ls.at[3]),
        pltpu.make_async_copy(inputs, inp, ls.at[4]),
        pltpu.make_async_copy(weights, wts, ls.at[5]),
    ]
    for n in (0, 3, 4, 5, 1, 2):
        loads[n].start()

    groups, total_sent = [], [0]

    def group(size=1):
        groups.append([0, size, sum(g[1] for g in groups)])
        return groups[-1]

    def send(src, dst, dev, g, at=0):
        size = math.prod(src.shape) * src.dtype.itemsize
        g[0] += size
        total_sent[0] += size
        pltpu.make_async_remote_copy(
            src_ref=src, dst_ref=dst, send_sem=ss.at[0], recv_sem=rs.at[g[2] + at], device_id=dev, device_id_type=MESH
        ).start()

    def whole(size, at):
        ref = span.at[pl.ds(0, size // 512)]
        return pltpu.make_async_remote_copy(
            src_ref=ref, dst_ref=ref, send_sem=ss.at[0], recv_sem=rs.at[at], device_id=side, device_id_type=MESH
        )

    def arrived(g, at=0, parts=1):
        whole(g[0] // parts, g[2] + at).wait_recv()

    def lanes(at, size):
        return pl.ds(pl.multiple_of(at, 128), size)

    near = lanes((c * 2 + e) * quarter, quarter)
    far = lanes((c * 2 + 1 - e) * quarter, quarter)
    mine = lanes(c * half, half)
    first = (quarter // 128 + 1) // 2 * 128
    near_a = lanes((c * 2 + e) * quarter, first)
    far_b = lanes((c * 2 + 1 - e) * quarter + first, quarter - first)

    class Gather:
        def __init__(self, buf, direct):
            self.buf = buf
            self.direct = direct
            self.z, self.y, self.x, self.own = group(n_a), group(n_a), group(n_a), group()
            self.own_x, self.both, self.s0, self.s1 = group(), group(), group(), group()

        def start(self):
            buf = self.buf
            for p in reversed(others):
                k = far_slot[p]
                send(buf.at[0, 0, :, near], buf.at[0, k, :, near], (ups[p] * 2 + b, t), self.z, k)

        def own_side(self):
            send(self.buf.at[0, 0, :, near], self.buf.at[1, 0, :, near], side, self.own)

        def spread(self, which):
            buf = self.buf
            for p in which:
                k = near_slot[p]
                arrived(self.z, k, n_a - 1)
                send(buf.at[0, k, :, near], buf.at[0, k, :, near], across, self.x, p)
                send(buf.at[0, k, :, near], buf.at[1, k, :, near], side, self.y, p)
                if p in self.direct:
                    send(buf.at[0, k, :, near], buf.at[1, k, :, near], diag, self.both)

        def own_across(self):
            buf = self.buf
            arrived(self.own)
            send(buf.at[1, 0, :, near], buf.at[1, 0, :, near], across, self.both)

        def cross(self):
            buf = self.buf
            for p in others:
                k = near_slot[p]
                arrived(self.x, p, n_a - 1)
                if p not in self.direct:
                    send(buf.at[0, k, :, far_b], buf.at[1, k, :, far_b], side, self.both)
                arrived(self.y, p, n_a - 1)
                if p not in self.direct:
                    send(buf.at[1, k, :, near_a], buf.at[1, k, :, near_a], across, self.both)

        def share(self):
            buf = self.buf
            send(buf.at[0, 1:n_a, :, mine], buf.at[0, 1:n_a, :, mine], sib, self.s0)
            send(buf.at[1, :, :, near], buf.at[1, :, :, near], sib, self.s0)

        def close(self):
            buf = self.buf
            arrived(self.both)
            send(buf.at[1, :, :, far], buf.at[1, :, :, far], sib, self.s1)

    hidden, embed = Gather(hb, range(n_a // 2, n_a)), Gather(eb, ())
    pl.semaphore_wait(barrier, len(greet))
    loads[0].wait()
    hidden.start()
    hidden.own_side()
    aligned = cols % 128 == 0
    shared, squashed = group(), group()
    if aligned:
        for u in range(n_x):
            send(table.at[:, lanes((2 * u + 1 - c) * cols, cols)], tabs.at[u], sib, shared)
    else:
        send(table, tabs.at[0], sib, shared)
    for n in (3, 4, 5):
        loads[n].wait()
    ma[0, 0] = jnp.zeros(ma.shape[2:], f32)
    ma[0, 0, :, 0:rows] = tgt[...].astype(f32)
    ma[0, 0, :, rows:2 * rows] = inp[...].astype(f32)
    ma[0, 0, :, 2 * rows:3 * rows] = wts[...].astype(f32)
    hidden.spread(others)
    hidden.own_across()
    loads[1].wait()
    embed.start()
    embed.own_side()
    hidden.cross()
    hidden.share()
    facts = group()
    for i in range(2):
        for p in reversed(range(n_a)):
            if i + p:
                dev = (ups[p] * 2 + (1 - b if i else b), t)
                send(ma.at[0, 0], ma.at[i, far_slot[p]], dev, facts)
    loads[2].wait()
    piece = min(vocab, 256)

    def product(i, part, core):
        at = pl.ds(i * piece, piece)
        part_lanes = lanes((core * 2 + part) * quarter, quarter)
        return at, lax.dot_general(
            tab[at, part_lanes], hb[:, :, :, part_lanes].reshape(tokens, quarter), LANES, preferred_element_type=f32
        )

    def quarters(part, core, fresh=False):
        for i in range(vocab // piece):
            at, value = product(i, part, core)
            sq[0, at, :] = value if fresh else sq[0, at, :] + value

    def last(i, total):
        at, value = product(i, 1 - e, 1 - c)
        squash = jnp.tanh((sq[0, at, :] + value) / 30.0)
        sq[0, at, :] = squash
        return total + jnp.sum(jnp.exp(30.0 * squash), axis=0, keepdims=True)

    quarters(e, c, True)
    hidden.close()
    embed.spread(others[:2])
    quarters(1 - e, c)
    arrived(hidden.s0)
    quarters(e, 1 - c)
    arrived(hidden.s1)
    part = jnp.zeros((1, tokens), f32)
    for i in range(vocab // piece):
        part = last(i, part)

    lane = lax.rem(lax.broadcasted_iota(jnp.int32, (1, tokens), 1), tokens // 2)
    for i in range(2):
        for j in range(n_a):
            move = j * rows
            value = part
            if i:
                value = pltpu.roll(value, tokens // 2, 1)
            if j:
                value = jnp.where(
                    lane < tokens // 2 - move,
                    pltpu.roll(value, tokens - move, 1),
                    pltpu.roll(value, tokens // 2 - move, 1),
                )
            sv[i * n_a + j] = value
    sums = group()
    for p in reversed(range(n_a)):
        for i in reversed(range(2)):
            for u in reversed(range(n_x)):
                for k in reversed(range(2)):
                    n = ((i * n_a + p) * n_x + u) * 2 + k
                    if n:
                        dev = (ups[p] * 2 + (1 - b if i else b), xs[u] * 2 + (1 - c if k else c))
                        row = sv.at[i * n_a + near_slot[p]]
                        send(row, sd.at[((i * n_a + far_slot[p]) * n_x + (n_x - u) % n_x) * 2 + k], dev, sums)
    sd[0] = part
    send(sq.at[0], sq.at[1], sib, squashed)
    embed.own_across()
    embed.spread(others[2:])
    arrived(facts)
    for i in range(2):
        for j in range(n_a):
            k = i * n_a + j
            for f in range(3):
                ids[f:f + 1, k * rows:(k + 1) * rows] = ma[i, j, :, f * rows:(f + 1) * rows]
    base = (d * n_t + t) * vocab
    column = (base + lax.broadcasted_iota(jnp.int32, (vocab, tokens), 0)).astype(f32)
    lhs[:, tokens:] = jnp.where(column == ids[1:2, :], 1.0, 0.0).astype(bf16)
    embed.cross()
    embed.share()
    arrived(squashed)
    arrived(shared)
    arrived(sums)
    total = jnp.sum(sd[...], axis=0)
    shift = ((1 - 2 * c) * vocab).astype(f32)
    for k in range(2):
        squash = sq[k]
        hits = jnp.where(column == ids[0:1, :] - k * shift, 1.0, 0.0)
        dlogit = ids[2:3, :] * (jnp.exp(30.0 * squash) / total - hits) * (1.0 - squash * squash)
        if k == 0:
            lhs[:, :tokens] = dlogit.astype(bf16)
        dlt[k] = jnp.transpose(dlogit).astype(bf16)

    cut = min((cols // 128 + 1) // 2 * 128, cols) if aligned else cols
    split = cut < cols
    back = tokens // 2

    def pair(mine, theirs):
        return jnp.dot(dlt[0], mine, preferred_element_type=f32) + jnp.dot(dlt[1], theirs, preferred_element_type=f32)

    def term(u, start, stop):
        if aligned:
            at = lanes((2 * xs[u] + c) * cols + start, stop - start)
            return pair(tab[:, at], tabs[xs[u], :, start:stop])
        wide = jnp.zeros((tokens, cols), f32)
        for n in range(n_t):
            at = slice(n * cols, (n + 1) * cols)
            wide = jnp.where(2 * xs[u] + c == n, pair(tab[:, at], tabs[0, :, at]), wide)
        return wide

    order = list(range(1, n_x)) + [0]
    steps = list(reversed(range(n_a)))
    xa1, xa0, yb1, y2a, x2b = [[group() for p in range(n_a)] for n in range(5)]
    yb0, z3 = group(), group()

    def block(p, i=0):
        return pl.ds(i * back + pl.multiple_of(near_slot[p] * rows, rows) if p else i * back, rows)

    def send_x(p, i, g):
        for u in order[:-1]:
            at = block(p, i)
            send(qa.at[u, at], ra.at[n_x - u, at], (d, xs[u] * 2 + c), g)

    for u in order[:-1]:
        qa[u] = term(u, 0, cut).astype(bf16)
    for p in steps:
        send_x(p, 1, xa1[p])
    for u in order:
        if split:
            value = term(u, cut, cols)
            qb[u] = value[back:].astype(bf16)
            pf[u, :back, cut:] = value[:back]
        if split and u == order[-2]:
            for p in steps:
                for v in order[:-1]:
                    send(qb.at[v, block(p)], rb.at[v, block(p)], side, yb1[p])
    for p in steps[:2]:
        send_x(p, 0, xa0[p])
    if split:
        send(qb.at[0], rb.at[0], side, yb0)
    pf[0, :, :cut] = term(0, 0, cut)
    step = 256 if width % 256 == 0 else 128

    def table_cols(start, stop):
        for i in range(start, stop):
            at = slice(i * step, (i + 1) * step)
            both = gb[:, :, :, :, at].reshape(2 * tokens, step)
            head = jnp.dot(lhs[:, :tokens], both[:tokens], preferred_element_type=f32)
            tail = jnp.dot(lhs[:, tokens:], both[tokens:], preferred_element_type=f32)
            tg[:, at] = (head + scale * tail).astype(bf16)

    def over_x(p, i):
        at = block(p, i)
        value = pf[0, at, :cut]
        for u in range(1, n_x):
            value = value + ra[u, at].astype(f32)
        return value

    for n, p in enumerate(steps):
        at = block(p)
        arrived(xa1[p])
        q2a[at] = over_x(p, 1).astype(bf16)
        send(q2a.at[at], r2a.at[at], side, y2a[p])
        if split:
            arrived(yb1[p])
            for u in order[:-1]:
                q2b[u, at] = (pf[u, at, cut:] + rb[u, at].astype(f32)).astype(bf16)
                send(q2b.at[u, at], r2b.at[n_x - u, at], (d, xs[u] * 2 + c), x2b[p])
        if n + 2 < n_a:
            send_x(steps[n + 2], 0, xa0[steps[n + 2]])
    embed.close()
    tiles = width // step
    if split:
        arrived(yb0)
    for p in steps:
        at = block(p)
        arrived(xa0[p])
        value = over_x(p, 0)
        arrived(y2a[p])
        value = value + r2a[at].astype(f32)
        if p:
            q3a[p] = value.astype(bf16)
            send(q3a.at[p], r3a.at[far_slot[p]], (ups[p] * 2 + b, t), z3)
        else:
            hg[:, :cut] = value
        if split:
            value = pf[0, at, cut:] + rb[0, at].astype(f32)
            arrived(x2b[p])
            for u in range(1, n_x):
                value = value + r2b[u, at].astype(f32)
            if p:
                q3b[p] = value.astype(bf16)
                send(q3b.at[p], r3b.at[far_slot[p]], (ups[p] * 2 + b, t), z3)
            else:
                hg[:, cut:] = value
    arrived(embed.s0)
    arrived(embed.s1)
    table_cols(0, tiles)
    arrived(z3)
    value = hg[:, :cut]
    for j in others:
        value = value + r3a[j].astype(f32)
    hg[:, :cut] = value
    if split:
        value = hg[:, cut:]
        for j in others:
            value = value + r3b[j].astype(f32)
        hg[:, cut:] = value
    whole(total_sent[0], 0).wait_send()


def write(tg, hg, tg_out, hg_out, sems):
    copies = [pltpu.make_async_copy(tg, tg_out, sems.at[0]), pltpu.make_async_copy(hg, hg_out, sems.at[1])]
    for copy in copies:
        copy.start()
    for copy in copies:
        copy.wait()


def per_device(n_dp, n_t, hidden, tied_table, targets, loss_weight, inputs, embed_grad):
    rows, width = hidden.shape
    vocab = tied_table.shape[0]
    tokens, cols, n_x, n_a = n_dp * rows, width // n_t, n_t // 2, n_dp // 2
    f32, bf16 = jnp.float32, jnp.bfloat16
    vmem, hbm = pl.BlockSpec(memory_space=pltpu.VMEM), pl.BlockSpec(memory_space=pl.ANY)
    cut = min((cols // 128 + 1) // 2 * 128, cols) if cols % 128 == 0 else cols
    rest = cols - cut or 128
    receives = 2 * (3 * n_a + 5) + 4 + 5 * n_a + 2
    grads = pl.pallas_call(
        functools.partial(kernel, n_dp, n_t, math.sqrt(width)),
        out_shape=(
            pltpu.VMEM((vocab, width), bf16),
            pltpu.VMEM((rows, cols), f32),
        ),
        in_specs=[hbm] * 6,
        out_specs=(vmem, vmem),
        scratch_shapes=[
            pltpu.VMEM((1, rows), jnp.int32),
            pltpu.VMEM((1, rows), jnp.int32),
            pltpu.VMEM((1, rows), bf16),
            pltpu.VMEM((2, 2, n_a, rows, width), bf16),
            pltpu.VMEM((2, n_a, 1, 128), f32),
            pltpu.VMEM((8, tokens), f32),
            pltpu.VMEM((vocab, width), bf16),
            pltpu.VMEM((n_x, vocab, cols) if cols % 128 == 0 else (1, vocab, width), bf16),
            pltpu.VMEM((2, vocab, tokens), f32),
            pltpu.VMEM((vocab, 2 * tokens), bf16),
            pltpu.VMEM((2, tokens, vocab), bf16),
            pltpu.VMEM((n_dp, 1, tokens), f32),
            pltpu.VMEM((n_dp * n_t, 1, tokens), f32),
            pltpu.VMEM((n_x, tokens, cols), f32),
            pltpu.VMEM((n_x, tokens, cut), bf16),
            pltpu.VMEM((n_x, tokens, cut), bf16),
            pltpu.VMEM((n_x, tokens // 2, rest), bf16),
            pltpu.VMEM((n_x, tokens // 2, rest), bf16),
            pltpu.VMEM((tokens // 2, cut), bf16),
            pltpu.VMEM((tokens // 2, cut), bf16),
            pltpu.VMEM((n_x, tokens // 2, rest), bf16),
            pltpu.VMEM((n_x, tokens // 2, rest), bf16),
            pltpu.VMEM((n_a, rows, cut), bf16),
            pltpu.VMEM((n_a, rows, cut), bf16),
            pltpu.VMEM((n_a, rows, rest), bf16),
            pltpu.VMEM((n_a, rows, rest), bf16),
            pltpu.VMEM((tokens * width // 32, 1, 128), f32),
            pltpu.SemaphoreType.DMA((1,)),
            pltpu.SemaphoreType.DMA((receives,)),
            pltpu.SemaphoreType.DMA((6,)),
        ],
        compiler_params=pltpu.CompilerParams(
            collective_id=0, has_side_effects=True, vmem_limit_bytes=56 << 20
        ),
    )(targets[None], inputs[None], loss_weight[None], hidden, embed_grad, tied_table)
    return pl.pallas_call(
        write,
        out_shape=(jax.ShapeDtypeStruct((vocab, width), bf16), jax.ShapeDtypeStruct((rows, cols), f32)),
        in_specs=[vmem] * 2,
        out_specs=(hbm, hbm),
        scratch_shapes=[pltpu.SemaphoreType.DMA((2,))],
        compiler_params=pltpu.CompilerParams(vmem_limit_bytes=1 << 20),
    )(*grads)


def solution(mesh):
    placed = (P("dp", None), P(("dp", "tensor"), None), P("dp"), P("dp"), P("dp"), P("dp", None))
    return jax.shard_map(
        functools.partial(per_device, mesh.shape["dp"], mesh.shape["tensor"]),
        mesh=mesh,
        in_specs=placed,
        out_specs=(P(("dp", "tensor"), None), P("dp", "tensor")),
        check_vma=False,
    )
```
